512 devices in a mesh: expert: 128 (over z, y, core), tensor: 4 (over x).
Axes of the slice: x: 4, y: 4, z: 16, core: 2. Of those that a mesh axis runs over, the one named last changes fastest.
Arguments:
- tokens: bfloat16 [4096, 1536], P('expert')
- attn_gain: bfloat16 [1536], replicated, may hold values from 0.099609375 to 1.8984375
- query_weight: bfloat16 [1536, 1536], P(None, 'tensor'), may hold values from -0.15625 to 0.15625
- key_value_weight: bfloat16 [4, 1536, 128], P('tensor'), may hold values from -0.15625 to 0.15625
- paired_cache: bfloat16 [128, 4, 768, 128], P('expert', 'tensor')
- prompt_length: int32 [128, 3], P('expert'), may hold values from 1 to 256, 640 in all within a row
- group_index: int32 [4096], P('expert'), may hold values from 0 to 2
- offsets: int32 [4096], P('expert'), may hold values from 0 to 127
- sink_logit: float32 [12], P('tensor'), may hold values from -2 to 4
- out_weight: bfloat16 [1536, 1536], P('tensor'), may hold values from -0.15625 to 0.15625
- mixer_gain: bfloat16 [1536], replicated, may hold values from 0.099609375 to 1.8984375
- routes: int32 [4096, 4], P('expert'), may hold values from 0 to 31, all different within a row; in each aligned block of 8 rows (0 to 7, 8 to 15, ...) at most 2 rows name the same one
- route_weight: float32 [4096, 4], P('expert'), may hold values from 0.05 to 1
- copy_slot: int32 [128], replicated, may hold values from 0 to 127, as said below
- gate_weight: bfloat16 [128, 1536, 768], P('expert', None, 'tensor'), as said below
- up_weight: bfloat16 [128, 1536, 768], P('expert', None, 'tensor'), as said below
- down_weight: bfloat16 [128, 768, 1536], P('expert', 'tensor'), as said below
- final_gain: bfloat16 [1536], P('tensor'), may hold values from 0.099609375 to 1.8984375
Outputs:
- normed: bfloat16 [4096, 1536], P('expert', 'tensor')
The draws below stay inside these ranges and needn't reach their ends.
Inputs may be any that keep to these rules, and one draw needn't show every extreme that they name: `routes`: in each aligned block of 8 rows no expert is named by more than 2 rows, and in some block one is named by exactly 2. `copy_slot`: a permutation: every slot appears once; slot s lies on expert-axis index s // 1 as its local copy s % 1. `prompt_length`: on every expert-axis index one prompt fills all 256 slots. `gate_weight`: all 4 replicas of an expert hold equal weights. `up_weight`: all 4 replicas of an expert hold equal weights. `down_weight`: all 4 replicas of an expert hold equal weights.
All inputs are finite; a program needn't handle non-finite values.
Results may differ from the reference program's by a relative error of at most 0.013.
Values may be sent and summed in bfloat16 or wider, within the bound.
A program may use at most 64 MiB of HBM per device.

```python
import math
import jax
import jax.numpy as jnp
import numpy as np
from jax import lax

MODEL_WIDTH = 1536
QUERY_HEADS = 12
KEY_VALUE_HEADS = 2
HEAD_SIZE = 128
EXPERTS = 32
FF = 768
TOP = 4
TOK_DEV = 32
PROMPTS_DEV = 3
PROMPT_CAP = 256
GEN = 128
WINDOW = 192
TOKENS = 4096
CACHE_PER_SLICE = 768
COPIES = 128
REPL = 4
MOST = 2
N_EXPERT = 128
N_TENSOR = 4


def draw_tokens(key, part):
    first_key, second_key = jax.random.split(key)
    columns = 10.0 ** (jnp.arange(MODEL_WIDTH, dtype=jnp.float32) / MODEL_WIDTH)
    row_scale = 10.0 ** jax.random.uniform(second_key, (TOKENS, 1), jnp.float32)
    drawn_draw = jax.random.normal(first_key, (TOKENS, MODEL_WIDTH), jnp.float32)
    return (drawn_draw * columns[None, :] * row_scale / 8.0).astype(jnp.bfloat16)


def draw_paired_cache(key, part):
    first_key = jax.random.fold_in(key, 0)
    cache_layout = (N_EXPERT, 2 * KEY_VALUE_HEADS, CACHE_PER_SLICE, HEAD_SIZE)
    return jax.random.normal(first_key, cache_layout, jnp.float32).astype(jnp.bfloat16)


def slot_order(key):
    return jax.random.permutation(jax.random.fold_in(key, 7), COPIES).astype(jnp.int32)


def expert_of_slot(key):
    return (jnp.argsort(slot_order(key)) // REPL).astype(jnp.int32)


def draw_copy_slot(key, part):
    return slot_order(key)


def draw_gate_weight(key, part):
    drawn_draw = jax.random.normal(jax.random.fold_in(key, 11), (EXPERTS, MODEL_WIDTH, FF), jnp.float32) * MODEL_WIDTH ** (-0.5)
    return drawn_draw[expert_of_slot(key)].astype(jnp.bfloat16)


def draw_up_weight(key, part):
    drawn_draw = jax.random.normal(jax.random.fold_in(key, 13), (EXPERTS, MODEL_WIDTH, FF), jnp.float32) * MODEL_WIDTH ** (-0.5)
    return drawn_draw[expert_of_slot(key)].astype(jnp.bfloat16)


def draw_down_weight(key, part):
    drawn_draw = jax.random.normal(jax.random.fold_in(key, 17), (EXPERTS, FF, MODEL_WIDTH), jnp.float32) * FF ** (-0.5)
    return drawn_draw[expert_of_slot(key)].astype(jnp.bfloat16)


def set_ends(values, own_key, smallest, largest):
    shape = values.shape
    spot = [jax.random.randint(jax.random.fold_in(own_key, axis), (), 0, shape[axis]) for axis in range(len(shape))]
    values = values.at[tuple(spot)].set(smallest)
    longest = shape.index(max(shape))
    spot[longest] = (spot[longest] + 1) % shape[longest]
    return values.at[tuple(spot)].set(largest)


def levels(own_key, shape, cuts, least, largest):
    factor_of = 1.0
    for axis_at, blocks in cuts:
        draws = jax.random.uniform(jax.random.fold_in(jax.random.fold_in(own_key, 6), axis_at), (blocks,), jnp.float32, least / len(cuts), largest / len(cuts))
        factor_of = factor_of * jnp.repeat(jnp.exp(draws), shape[axis_at] // blocks).reshape((-1,) + (1,) * (len(shape) - 1 - axis_at))
    return factor_of


def profile(amount, total, limit, lean):
    loads = [(1 << 20) // math.isqrt(grade ** lean) + 1 for grade in range(2, amount + 1)]
    surplus, counts = total - limit - (amount - 1), [1] * (amount - 1)
    while surplus > 0:
        free = [i for i in range(amount - 1) if counts[i] < limit]
        whole, left = sum([loads[i] for i in free]), surplus
        for i in free:
            more = min(limit - counts[i], max(1, left * loads[i] // whole), surplus)
            counts[i] = counts[i] + more
            surplus = surplus - more
    return np.array([limit] + counts)


def ragged_sizes(stream_key, number_of, total, limit, skew):
    if number_of == 2:
        one = jax.random.randint(stream_key, (), max(1, total - limit), min(limit, total - 1) + 1)
        return jnp.stack([one, total - one])
    sizes = jnp.asarray(profile(number_of, total, limit, skew), jnp.int32)
    couples = (number_of - 1) // 2
    giver, sink = sizes[1:1 + 2 * couples:2], sizes[2:2 + 2 * couples:2]
    slack = jnp.minimum(giver - 1, limit - sink)
    shifted = jax.random.randint(jax.random.fold_in(stream_key, 1), (couples,), 0, 1 << 20) % (slack + 1)
    sizes = sizes.at[1:1 + 2 * couples:2].set(giver - shifted).at[2:2 + 2 * couples:2].set(sink + shifted)
    return sizes[jax.random.permutation(jax.random.fold_in(stream_key, 2), number_of)]


def routed_block(stream_key, own, number, rows, count, top, most, slope):
    order = jax.random.permutation(stream_key, count)
    packed, common = load_shares(count, rows * top, most, slope, True), load_shares(count, rows * top, most, slope, False)
    places = jnp.arange(count)

    def named(sizes, turn):
        used = int((sizes > 0).sum())
        fixed = max(1, used // 4)
        shifted = fixed + (places - fixed + turn * (used - fixed)) % max(1, count - fixed)
        return jnp.zeros((count,), jnp.int32).at[order[jnp.where(places < fixed, places, shifted)]].set(jnp.asarray(sizes, jnp.int32))

    sizes = jnp.where(number % 4 == 0, named(packed, number // 4), named(common, number - number // 4 - 1))
    mixed = jax.random.permutation(jax.random.fold_in(own, 3), count)
    giver, receiver = mixed[0:count // 2 * 2:2], mixed[1:count // 2 * 2:2]
    margin = jnp.minimum(sizes[giver] - 1, most - sizes[receiver]) // 2
    margin = jnp.where((giver == order[0]) | (receiver == order[0]) | (sizes[receiver] == 0), 0, jnp.maximum(margin, 0))
    shifted = jax.random.randint(jax.random.fold_in(own, 4), (count // 2,), 0, 1 << 20) % (margin + 1)
    sizes = sizes.at[giver].add(-shifted).at[receiver].add(shifted)
    items = jnp.searchsorted(jnp.cumsum(sizes), jnp.arange(rows * top), side="right").astype(jnp.int32)
    table = items.reshape(top, rows).T
    table = table[jax.random.permutation(jax.random.fold_in(own, 1), rows)]
    turn = jax.random.randint(jax.random.fold_in(own, 2), (rows, 1), 0, top)
    return jnp.take_along_axis(table, (jnp.arange(top)[None, :] + turn) % top, axis=1)


def load_shares(amount, total, limit, skew, full):
    weights = [(1 << 20) // math.isqrt(grade ** skew) + 1 for grade in range(1, amount + 1)]
    largest = limit if full else min(limit, max(-(-total // amount), total * weights[0] // sum(weights)))
    least = 1 if total - largest >= amount - 1 else 0
    holding, spare = [largest] + [least] * (amount - 1), total - largest - least * (amount - 1)
    while spare > 0:
        candidates = [i for i in range(1, amount) if holding[i] < largest] or [i for i in range(1, amount) if holding[i] < limit]
        whole, remaining = sum([weights[i] for i in candidates]), spare
        for i in candidates:
            extra = min(limit - holding[i], max(1, remaining * weights[i] // whole), spare)
            holding[i] = holding[i] + extra
            spare = spare - extra
    return np.array(holding)


def normal_values(own_key, extent, scale, bound, cuts=(), kind=jnp.bfloat16):
    level = levels(own_key, extent, cuts, -0.22, 0.18) if cuts else 1.0
    result = jax.random.normal(own_key, extent, jnp.float32) * scale * level
    return jnp.minimum(jnp.maximum(result, -bound), bound).astype(kind)


def setup_inputs(seed: int = 0) -> dict:
    arg_keys = jax.random.split(jax.random.key(seed), 19)
    tokens = draw_tokens(jax.random.fold_in(arg_keys[18], 71), 0)
    attn_gain = jnp.clip(1.0 + 0.18 * jax.random.normal(arg_keys[1], (MODEL_WIDTH,), jnp.float32), 0.099609375, 1.8984375).astype(jnp.bfloat16)
    query_weight = normal_values(arg_keys[2], (MODEL_WIDTH, QUERY_HEADS * HEAD_SIZE), MODEL_WIDTH ** -0.5, 0.15625, ((1, 4),))
    key_value_weight = normal_values(arg_keys[3], (2 * KEY_VALUE_HEADS, MODEL_WIDTH, HEAD_SIZE), MODEL_WIDTH ** -0.5, 0.15625, ((0, 4),))
    paired_cache = draw_paired_cache(jax.random.fold_in(arg_keys[18], 71), 0)
    prompt_length = jax.vmap(lambda own: ragged_sizes(own, PROMPTS_DEV, PROMPTS_DEV * PROMPT_CAP * 5 // 6, PROMPT_CAP, 1))(jax.random.split(arg_keys[5], N_EXPERT)).reshape((N_EXPERT, PROMPTS_DEV)).astype(jnp.int32)
    group_index = set_ends(jax.random.randint(arg_keys[6], (TOKENS,), 0, PROMPTS_DEV), jax.random.fold_in(arg_keys[6], 1), 0, PROMPTS_DEV - 1).astype(jnp.int32)
    offsets = set_ends(jax.random.randint(arg_keys[7], (TOKENS,), 0, GEN), jax.random.fold_in(arg_keys[7], 1), 0, GEN - 1).astype(jnp.int32)
    sink_logit = jnp.clip(-2.0 + 6.0 * jax.random.uniform(arg_keys[8], (QUERY_HEADS,), jnp.float32) ** levels(arg_keys[8], (QUERY_HEADS,), ((0, 4),), -0.2, 0.2), -2.0, 4.0)
    out_weight = normal_values(arg_keys[9], (QUERY_HEADS * HEAD_SIZE, MODEL_WIDTH), (QUERY_HEADS * HEAD_SIZE) ** -0.5, 0.15625, ((0, 4),))
    mixer_gain = jnp.clip(1.0 + 0.18 * jax.random.normal(arg_keys[10], (MODEL_WIDTH,), jnp.float32), 0.099609375, 1.8984375).astype(jnp.bfloat16)
    routes_keys = jax.random.split(jax.random.fold_in(arg_keys[11], 1), TOKENS // (TOK_DEV // REPL))
    routes_turns = jax.random.permutation(jax.random.fold_in(arg_keys[11], 3), TOKENS // (TOK_DEV // REPL))
    routes = jax.vmap(lambda own, number: routed_block(jax.random.fold_in(arg_keys[11], 2), own, number, TOK_DEV // REPL, EXPERTS, TOP, MOST, 2))(routes_keys, routes_turns).reshape((TOKENS, TOP))
    route_weight = jnp.clip(jnp.exp(math.log(1.0) - 2.9957323 * jax.random.uniform(arg_keys[12], (TOKENS, TOP), jnp.float32) ** levels(arg_keys[12], (TOKENS, TOP), ((0, 128),), -0.2, 0.2)), 0.05, 1.0)
    copy_slot = draw_copy_slot(jax.random.fold_in(arg_keys[18], 71), 0)
    gate_weight = draw_gate_weight(jax.random.fold_in(arg_keys[18], 71), 0)
    up_weight = draw_up_weight(jax.random.fold_in(arg_keys[18], 71), 0)
    down_weight = draw_down_weight(jax.random.fold_in(arg_keys[18], 71), 0)
    final_gain = jnp.clip(1.0 + 0.18 * jax.random.normal(arg_keys[17], (MODEL_WIDTH,), jnp.float32), 0.099609375, 1.8984375).astype(jnp.bfloat16)
    return {"tokens": tokens, "attn_gain": attn_gain, "query_weight": query_weight, "key_value_weight": key_value_weight, "paired_cache": paired_cache, "prompt_length": prompt_length, "group_index": group_index, "offsets": offsets, "sink_logit": sink_logit, "out_weight": out_weight, "mixer_gain": mixer_gain, "routes": routes, "route_weight": route_weight, "copy_slot": copy_slot, "gate_weight": gate_weight, "up_weight": up_weight, "down_weight": down_weight, "final_gain": final_gain}


EPSILON = 1e-06

def rms_scale(values, gain_row):
    mean_square = lax.optimization_barrier(jnp.mean(values * values, axis=-1, keepdims=True))
    return values * lax.rsqrt(mean_square + EPSILON) * gain_row.astype(jnp.float32)

def rotate(values, position):
    half_dim = values.shape[-1] // 2
    frequency = 10000.0 ** (-jnp.arange(half_dim, dtype=jnp.float32) / half_dim)
    angles = position.astype(jnp.float32)[:, None] * frequency[None, :]
    if values.ndim == 3:
        angles = angles[:, None, :]
    cosine_part = jnp.cos(angles)
    sine_part = jnp.sin(angles)
    front_half = values[..., :half_dim]
    back_half = values[..., half_dim:]
    return jnp.concatenate([front_half * cosine_part - back_half * sine_part, front_half * sine_part + back_half * cosine_part], axis=-1)

def slot_places(routes, copy_slot, replicas):
    row_count = routes.shape[0]
    flat_routes = routes.reshape(-1)
    slot_count = flat_routes.shape[0]
    block_of = jnp.arange(slot_count, dtype=jnp.int32) // TOP // (row_count // replicas)
    onehot = (flat_routes[:, None] == jnp.arange(EXPERTS, dtype=jnp.int32)[None, :]).astype(jnp.int32)
    grouped = onehot.reshape(replicas, slot_count // replicas, EXPERTS)
    earlier = jnp.cumsum(grouped, axis=1) - grouped
    slot_rank = lax.optimization_barrier(jnp.sum(earlier * grouped, axis=-1)).reshape(slot_count)
    holder = copy_slot[flat_routes * replicas + block_of]
    return (holder, slot_rank)

def reference(tokens, attn_gain, query_weight, key_value_weight, paired_cache, prompt_length, group_index, offsets, sink_logit, out_weight, mixer_gain, routes, route_weight, copy_slot, gate_weight, up_weight, down_weight, final_gain):
    score_scale = 1.0 / HEAD_SIZE ** 0.5
    group_width = QUERY_HEADS // KEY_VALUE_HEADS

    def attend(inputs):
        rows_in, cache_block, lengths, groups, offset_rows = inputs
        normed_in = rms_scale(rows_in.astype(jnp.float32), attn_gain).astype(jnp.bfloat16)
        row_length = lengths[groups]
        position = row_length + offset_rows
        queries = jnp.dot(normed_in, query_weight, preferred_element_type=jnp.float32).reshape(-1, QUERY_HEADS, HEAD_SIZE)
        queries = rotate(queries, position).astype(jnp.bfloat16)
        projected = jnp.einsum('td,kde->tke', normed_in.astype(jnp.float32), key_value_weight.astype(jnp.float32))
        new_keys = rotate(projected[:, 0::2], position).astype(jnp.bfloat16)
        new_values = projected[:, 1::2].astype(jnp.bfloat16)
        new_keys = jnp.repeat(new_keys, group_width, axis=1)
        new_values = jnp.repeat(new_values, group_width, axis=1)
        cache_keys = jnp.repeat(cache_block[0::2], group_width, axis=0)
        cache_values = jnp.repeat(cache_block[1::2], group_width, axis=0)
        scores = jnp.einsum('thd,hcd->thc', queries.astype(jnp.float32), cache_keys.astype(jnp.float32)) * score_scale
        self_score = lax.optimization_barrier(jnp.sum(queries.astype(jnp.float32) * new_keys.astype(jnp.float32), axis=-1)) * score_scale
        slot_index = jnp.arange(CACHE_PER_SLICE, dtype=jnp.int32)
        slot_group = slot_index // PROMPT_CAP
        slot_pos = slot_index % PROMPT_CAP
        visible = (slot_group[None, :] == groups[:, None]) & (slot_pos[None, :] < row_length[:, None]) & (slot_pos[None, :] > position[:, None] - WINDOW)
        visible = visible[:, None, :]
        masked = jnp.where(visible, scores, -jnp.inf)
        ceiling = jnp.maximum(jnp.maximum(lax.optimization_barrier(jnp.max(masked, axis=-1)), self_score), sink_logit[None, :])
        weights = jnp.where(visible, jnp.exp(scores - ceiling[..., None]), 0.0)
        own_weight = jnp.exp(self_score - ceiling)
        denominator = lax.optimization_barrier(jnp.sum(weights, axis=-1)) + own_weight + jnp.exp(sink_logit[None, :] - ceiling)
        probabilities = (weights / denominator[..., None]).astype(jnp.bfloat16)
        own_prob = (own_weight / denominator).astype(jnp.bfloat16)
        context = jnp.einsum('thc,hcd->thd', probabilities.astype(jnp.float32), cache_values.astype(jnp.float32))
        context = context + own_prob.astype(jnp.float32)[..., None] * new_values.astype(jnp.float32)
        context = context.astype(jnp.bfloat16).reshape(-1, QUERY_HEADS * HEAD_SIZE)
        attended = jnp.dot(context, out_weight, preferred_element_type=jnp.float32)
        return (rows_in.astype(jnp.float32) + attended).astype(jnp.bfloat16)
    residual = lax.map(attend, (tokens.reshape(N_EXPERT, TOK_DEV, MODEL_WIDTH), paired_cache, prompt_length, group_index.reshape(N_EXPERT, TOK_DEV), offsets.reshape(N_EXPERT, TOK_DEV)))
    residual = residual.reshape(TOKENS, MODEL_WIDTH)
    mixed_in = rms_scale(residual.astype(jnp.float32), mixer_gain).astype(jnp.bfloat16)
    replicas = COPIES // EXPERTS

    def place_device(device_routes):
        return slot_places(device_routes, copy_slot, replicas)
    holders, slot_ranks = jax.vmap(place_device)(routes.reshape(N_EXPERT, TOK_DEV, TOP))
    copy_rows = N_EXPERT * MOST
    source = jnp.arange(N_EXPERT, dtype=jnp.int32)[:, None]
    places = (holders * copy_rows + source * MOST + slot_ranks).reshape(-1)
    slot_ids = jnp.arange(TOKENS * TOP, dtype=jnp.int32)
    slot_table = jnp.zeros((COPIES * copy_rows,), jnp.int32).at[places].set(slot_ids).reshape(COPIES, copy_rows)
    block_units = FF // N_TENSOR

    def expert_rows(inputs):
        slot_picks, gate_part, up_part, down_part = inputs
        gathered = mixed_in[slot_picks // TOP]
        gate_val = jnp.dot(gathered, gate_part, preferred_element_type=jnp.float32)
        up_val = jnp.dot(gathered, up_part, preferred_element_type=jnp.float32)
        hidden = (jnp.maximum(gate_val, 0.0) * up_val).astype(jnp.bfloat16)
        partial_sums = jnp.einsum('rbf,bfd->brd', hidden.reshape(copy_rows, N_TENSOR, block_units).astype(jnp.float32), down_part.reshape(N_TENSOR, block_units, MODEL_WIDTH).astype(jnp.float32))
        rounded = lax.optimization_barrier(partial_sums.astype(jnp.bfloat16)).astype(jnp.float32)
        return lax.optimization_barrier(jnp.sum(rounded, axis=0)).astype(jnp.bfloat16)
    expert_out = lax.map(expert_rows, (slot_table, gate_weight, up_weight, down_weight)).reshape(COPIES * copy_rows, MODEL_WIDTH)
    per_slot = expert_out[places].astype(jnp.float32).reshape(TOKENS, TOP, MODEL_WIDTH)
    mixture = lax.optimization_barrier(jnp.sum(route_weight[..., None] * per_slot, axis=1))
    combined = residual.astype(jnp.float32) + mixture
    return rms_scale(combined, final_gain).astype(jnp.bfloat16)
```

```python
import jax
import jax.numpy as jnp
from jax import lax
from jax.experimental import pallas as pl
from jax.experimental.pallas import tpu as pltpu
from jax.sharding import PartitionSpec as P

EXPERTS = 32
TOP = 4
PROMPT_CAP = 256
WINDOW = 192


EPSILON = 1e-06


def from_partner(block, axis, apart):
    count = lax.axis_size(axis)
    route = []
    for low in range(count):
        high = low | 1 << apart
        if high != low and high < count:
            route += [(low, high), (high, low)]
    return lax.ppermute(block, axis, route)


def rms_scale(values, gain_row):
    mean_square = jnp.mean(values * values, axis=-1, keepdims=True)
    return values * lax.rsqrt(mean_square + EPSILON) * gain_row.astype(jnp.float32)


def rotate(values, position):
    half_dim = values.shape[-1] // 2
    frequency = 10000.0 ** (-jnp.arange(half_dim, dtype=jnp.float32) / half_dim)
    angles = position.astype(jnp.float32)[:, None] * frequency[None, :]
    if values.ndim == 3:
        angles = angles[:, None, :]
    cosine_part = jnp.cos(angles)
    sine_part = jnp.sin(angles)
    front_half = values[..., :half_dim]
    back_half = values[..., half_dim:]
    return jnp.concatenate(
        [
            front_half * cosine_part - back_half * sine_part,
            front_half * sine_part + back_half * cosine_part,
        ],
        axis=-1,
    )


def slot_places(routes, copy_slot):
    rows = routes.shape[0]
    copies = copy_slot.shape[0]
    replicas = copies // EXPERTS
    block = jnp.arange(rows, dtype=jnp.int32) // (rows // replicas)
    row = jnp.arange(rows, dtype=jnp.int32)
    earlier = (block[:, None] == block[None, :]) & (row[None, :] < row[:, None])
    same = routes[:, :, None, None] == routes[None, None, :, :]
    rank = jnp.sum((same & earlier[:, None, :, None]).astype(jnp.int32), axis=(2, 3))
    wanted = routes * replicas + block[:, None]
    picks = wanted[:, :, None] == jnp.arange(copies, dtype=jnp.int32)
    holder = jnp.sum(jnp.where(picks, copy_slot, 0), axis=-1)
    return (holder % PLANE) * (2 * RING) + (holder // PLANE) * 2 + rank


RING = 16
PLANE = 8
LANES = 4
PART = 384
MESH = pl.DeviceIdType.MESH


def far_first(t):
    half = (t + 1) // 2
    return RING // 2 + half * (1 - 2 * (t % 2))


def remote(src, dst, send, recv, expert, tensor):
    return pltpu.make_async_remote_copy(
        src_ref=src,
        dst_ref=dst,
        send_sem=send,
        recv_sem=recv,
        device_id=(expert, tensor),
        device_id_type=MESH,
    )


def dot(a, b):
    return jnp.dot(a, b, preferred_element_type=jnp.float32)


def moe_kernel(
    context_ref,
    out_weight_ref,
    tokens_ref,
    mixer_ref,
    places_ref,
    places_t_ref,
    route_weight_ref,
    gate_ref,
    up_ref,
    down_ref,
    final_ref,
    out_ref,
    att,
    att_in,
    sq,
    sq_in,
    plane_out,
    plane_in,
    ring_out,
    box,
    partial,
    partial_in,
    sums,
    sums_in,
    back_out,
    back_in,
    s_att,
    r_att,
    s_sq,
    r_sq,
    s_plane,
    r_plane,
    s_ring,
    r_ring,
    s_box,
    r_box,
    s_part,
    r_part,
    s_sum,
    r_sum,
    s_back,
    r_back,
):
    me = lax.axis_index("expert")
    x = lax.axis_index("tensor")
    z = me // PLANE
    yc = me % PLANE
    rows = tokens_ref.shape[0]
    width = LANES * PART

    barrier = pltpu.get_barrier_semaphore()

    def greet(expert, tensor):
        pl.semaphore_signal(barrier, inc=1, device_id=(expert, tensor), device_id_type=MESH)

    @pl.loop(1, RING)
    def _(d):
        greet((z + d) % RING * PLANE + yc, x)

    @pl.loop(1, PLANE)
    def _(d):
        greet(z * PLANE + (yc + d) % PLANE, x)

    @pl.loop(1, LANES)
    def _(d):
        greet(me, (x + d) % LANES)

    context = context_ref[...]
    for j in range(LANES):
        att[j] = dot(context, out_weight_ref[:, j * PART : (j + 1) * PART]).astype(jnp.bfloat16)
    pl.semaphore_wait(barrier, RING + PLANE + LANES - 3)

    def att_copy(d):
        to = (x + d) % LANES
        return remote(att.at[to], att_in.at[d - 1], s_att.at[d - 1], r_att.at[d - 1], me, to)

    for d in range(1, LANES):
        att_copy(d).start()
    mine = pl.ds(pl.multiple_of(x * PART, 128), PART)
    summed = att[x].astype(jnp.float32)
    for d in range(1, LANES):
        att_copy(d).wait_recv()
        summed = summed + att_in[d - 1].astype(jnp.float32)
    summed = summed.astype(jnp.bfloat16).astype(jnp.float32)
    residual = (tokens_ref[:, mine].astype(jnp.float32) + summed).astype(jnp.bfloat16)
    residual = residual.astype(jnp.float32)

    def whole_square(values, which):
        own = jnp.sum(values * values, axis=1, keepdims=True)
        sq[which] = jnp.broadcast_to(own, (rows, 128))

        def copy(d):
            to = (x + d) % LANES
            return remote(
                sq.at[which],
                sq_in.at[which, d - 1],
                s_sq.at[which, d - 1],
                r_sq.at[which, d - 1],
                me,
                to,
            )

        for d in range(1, LANES):
            copy(d).start()
        total = own
        for d in range(1, LANES):
            copy(d).wait_recv()
            total = total + sq_in[which, d - 1][:, :1]
        for d in range(1, LANES):
            copy(d).wait_send()
        return total

    total = whole_square(residual, 0)
    gain = mixer_ref[:, mine].astype(jnp.float32)
    mixed = (residual * lax.rsqrt(total / width + EPSILON) * gain).astype(jnp.bfloat16)

    slots = 2 * RING * PLANE
    place_row = lax.broadcasted_iota(jnp.int32, (slots, rows), 0)
    taken = jnp.zeros((slots, rows), jnp.float32)
    for k in range(TOP):
        taken = taken + (places_t_ref[k : k + 1, :] == place_row).astype(jnp.float32)
    outbox = dot(taken.astype(jnp.bfloat16), mixed).astype(jnp.bfloat16)
    plane_out[...] = outbox.reshape(PLANE, 2 * RING, PART)

    def plane_copy(d):
        to = (yc + d) % PLANE
        return remote(
            plane_out.at[to], plane_in.at[yc], s_plane.at[d], r_plane.at[d], z * PLANE + to, x
        )

    def plane_arrival(d):
        return remote(
            plane_out.at[yc],
            plane_in.at[(yc + PLANE - d) % PLANE],
            s_plane.at[d],
            r_plane.at[d],
            me,
            (x + 1) % LANES,
        )

    @pl.loop(1, PLANE)
    def _(d):
        plane_copy(d).start()

    plane_in[yc] = plane_out[yc]

    @pl.loop(1, PLANE)
    def _(d):
        plane_arrival(d).wait_recv()

    to_row = lax.broadcasted_iota(jnp.int32, (slots, slots), 0)
    from_row = lax.broadcasted_iota(jnp.int32, (slots, slots), 1)
    by_ring = ((to_row >> 1) & (PLANE - 1)) * (2 * RING) + (to_row >> 4) * 2 + (to_row & 1)
    by_ring = (by_ring == from_row).astype(jnp.float32).astype(jnp.bfloat16)
    by_plane = ((to_row >> 1) & (RING - 1)) * (2 * PLANE) + (to_row >> 5) * 2 + (to_row & 1)
    by_plane = (by_plane == from_row).astype(jnp.float32).astype(jnp.bfloat16)
    ordered = dot(by_ring, plane_in[...].reshape(slots, PART)).astype(jnp.bfloat16)
    ring_out[...] = ordered.reshape(RING, 2 * PLANE, PART)

    def ring_copy(d):
        to = (z + d) % RING
        return remote(
            ring_out.at[to], box.at[x, z], s_ring.at[d], r_ring.at[d], to * PLANE + yc, x
        )

    def ring_arrival(d):
        return remote(
            ring_out.at[z],
            box.at[x, (z + RING - d) % RING],
            s_ring.at[d],
            r_ring.at[d],
            me,
            (x + 1) % LANES,
        )

    def box_copy(d, j):
        at = (z + RING - d) % RING
        return remote(
            box.at[x, at],
            box.at[x, at],
            s_box.at[d, j - 1],
            r_box.at[d, j - 1],
            me,
            (x + j) % LANES,
        )

    def box_arrival(d, j):
        at = (z + RING - d) % RING
        return remote(
            box.at[x, at],
            box.at[(x + LANES - j) % LANES, at],
            s_box.at[d, j - 1],
            r_box.at[d, j - 1],
            me,
            (x + j) % LANES,
        )

    @pl.loop(0, RING - 1)
    def _(t):
        ring_copy(far_first(t)).start()

    box[x, z] = ring_out[z]
    for j in range(1, LANES):
        box_copy(0, j).start()

    @pl.loop(0, RING - 1)
    def _(t):
        d = far_first(t)
        ring_arrival(d).wait_recv()
        for j in range(1, LANES):
            box_copy(d, j).start()

    @pl.loop(0, RING)
    def _(d):
        for j in range(1, LANES):
            box_arrival(d, j).wait_recv()

    gate_val = jnp.zeros((slots, gate_ref.shape[1]), jnp.float32)
    up_val = jnp.zeros((slots, gate_ref.shape[1]), jnp.float32)
    for j in range(LANES):
        part = box[j].reshape(slots, PART)
        gate_val = gate_val + dot(part, gate_ref[j * PART : (j + 1) * PART, :])
        up_val = up_val + dot(part, up_ref[j * PART : (j + 1) * PART, :])
    hidden = (jnp.maximum(gate_val, 0.0) * up_val).astype(jnp.bfloat16)
    for j in range(LANES):
        product = dot(hidden, down_ref[:, j * PART : (j + 1) * PART]).astype(jnp.bfloat16)
        partial[j] = product.reshape(RING, 2 * PLANE, PART)

    def part_copy(d, j):
        at = (z + d) % RING
        to = (x + j) % LANES
        return remote(
            partial.at[to, at],
            partial_in.at[j - 1, at],
            s_part.at[d, j - 1],
            r_part.at[d, j - 1],
            me,
            to,
        )

    def sum_copy(d):
        to = (z + d) % RING
        return remote(sums.at[to], sums_in.at[z], s_sum.at[d], r_sum.at[d], to * PLANE + yc, x)

    def sum_arrival(d):
        return remote(
            sums.at[z],
            sums_in.at[(z + RING - d) % RING],
            s_sum.at[d],
            r_sum.at[d],
            me,
            (x + 1) % LANES,
        )

    @pl.loop(0, RING)
    def _(t):
        for j in range(1, LANES):
            part_copy(far_first(t), j).start()

    def add_parts(d):
        at = (z + d) % RING
        value = partial[x, at].astype(jnp.float32)
        for j in range(1, LANES):
            part_copy(d, j).wait_recv()
            value = value + partial_in[j - 1, at].astype(jnp.float32)
        return value.astype(jnp.bfloat16)

    @pl.loop(0, RING - 1)
    def _(t):
        d = far_first(t)
        sums[(z + d) % RING] = add_parts(d)
        sum_copy(d).start()

    sums_in[z] = add_parts(0)

    @pl.loop(1, RING)
    def _(d):
        sum_arrival(d).wait_recv()

    ordered = dot(by_plane, sums_in[...].reshape(slots, PART)).astype(jnp.bfloat16)
    back_out[...] = ordered.reshape(PLANE, 2 * RING, PART)

    def back_copy(d):
        to = (yc + d) % PLANE
        return remote(
            back_out.at[to], back_in.at[yc], s_back.at[d], r_back.at[d], z * PLANE + to, x
        )

    def back_arrival(d):
        return remote(
            back_out.at[yc],
            back_in.at[(yc + PLANE - d) % PLANE],
            s_back.at[d],
            r_back.at[d],
            me,
            (x + 1) % LANES,
        )

    @pl.loop(1, PLANE)
    def _(d):
        back_copy(d).start()

    back_in[yc] = back_out[yc]
    place_col = lax.broadcasted_iota(jnp.int32, (rows, slots), 1)
    weigh = jnp.zeros((rows, slots), jnp.float32)
    for k in range(TOP):
        hit = places_ref[:, k : k + 1] == place_col
        weigh = weigh + jnp.where(hit, route_weight_ref[:, k : k + 1], 0.0)
    high = weigh.astype(jnp.bfloat16)
    low = (weigh - high.astype(jnp.float32)).astype(jnp.bfloat16)

    @pl.loop(1, PLANE)
    def _(d):
        back_arrival(d).wait_recv()

    returned = back_in[...].reshape(slots, PART)
    combined = residual + (dot(high, returned) + dot(low, returned))
    total = whole_square(combined, 1)
    final = final_ref[...].astype(jnp.float32)
    out_ref[...] = (combined * lax.rsqrt(total / width + EPSILON) * final).astype(out_ref.dtype)

    for d in range(1, LANES):
        att_copy(d).wait_send()

    @pl.loop(1, PLANE)
    def _(d):
        plane_copy(d).wait_send()
        back_copy(d).wait_send()

    @pl.loop(1, RING)
    def _(d):
        ring_copy(d).wait_send()
        sum_copy(d).wait_send()

    @pl.loop(0, RING)
    def _(d):
        for j in range(1, LANES):
            box_copy(d, j).wait_send()
            part_copy(d, j).wait_send()


def moe_call(*operands):
    rows = operands[2].shape[0]
    vmem, sem = pltpu.VMEM, pltpu.SemaphoreType.DMA
    bf16 = jnp.bfloat16
    by_plane = vmem((PLANE, 2 * RING, PART), bf16)
    by_ring = vmem((RING, 2 * PLANE, PART), bf16)
    return pl.pallas_call(
        moe_kernel,
        out_shape=jax.ShapeDtypeStruct((rows, PART), bf16),
        in_specs=[pl.BlockSpec(memory_space=pltpu.VMEM)] * len(operands),
        out_specs=pl.BlockSpec(memory_space=pltpu.VMEM),
        scratch_shapes=[
            vmem((LANES, rows, PART), bf16),
            vmem((LANES - 1, rows, PART), bf16),
            vmem((2, rows, 128), jnp.float32),
            vmem((2, LANES - 1, rows, 128), jnp.float32),
            by_plane,
            by_plane,
            by_ring,
            vmem((LANES, RING, 2 * PLANE, PART), bf16),
            vmem((LANES, RING, 2 * PLANE, PART), bf16),
            vmem((LANES - 1, RING, 2 * PLANE, PART), bf16),
            by_ring,
            by_ring,
            by_plane,
            by_plane,
        ]
        + [sem((LANES - 1,))] * 2
        + [sem((2, LANES - 1))] * 2
        + [sem((PLANE,))] * 2
        + [sem((RING,))] * 2
        + [sem((RING, LANES - 1))] * 4
        + [sem((RING,))] * 2
        + [sem((PLANE,))] * 2,
        compiler_params=pltpu.CompilerParams(collective_id=0, has_side_effects=True),
    )(*operands)


def on_device(
    tokens,
    attn_gain,
    query_weight,
    key_value_weight,
    paired_cache,
    prompt_length,
    group_index,
    offsets,
    sink_logit,
    out_weight,
    mixer_gain,
    routes,
    route_weight,
    copy_slot,
    gate_weight,
    up_weight,
    down_weight,
    final_gain,
):
    lanes = lax.axis_size("tensor")
    member = lax.axis_index("tensor")
    peers = lax.axis_size("expert")
    tok_rows, width = tokens.shape
    head_dim = key_value_weight.shape[2]
    local_heads = query_weight.shape[1] // head_dim
    score_scale = 1.0 / head_dim**0.5
    rows_f32 = tokens.astype(jnp.float32)
    normed_in = rms_scale(rows_f32, attn_gain).astype(jnp.bfloat16)
    lengths = prompt_length[0]
    prompt_slots = jnp.arange(lengths.shape[0], dtype=jnp.int32)
    row_length = jnp.sum(
        jnp.where(group_index[:, None] == prompt_slots[None, :], lengths[None, :], 0), axis=1
    )
    position = row_length + offsets
    queries = jnp.dot(normed_in, query_weight, preferred_element_type=jnp.float32).reshape(
        tok_rows, local_heads, head_dim
    )
    queries = rotate(queries, position).astype(jnp.bfloat16)
    projected = jnp.dot(normed_in, key_value_weight[0], preferred_element_type=jnp.float32)
    marks_key = member % 2 == 0
    own_projection = jnp.where(marks_key, rotate(projected, position), projected).astype(
        jnp.bfloat16
    )
    own_cache = paired_cache[0, 0]
    partner, partner_cache = from_partner((own_projection, own_cache), "tensor", 0)
    new_keys = jnp.where(marks_key, own_projection, partner)
    new_values = jnp.where(marks_key, partner, own_projection)
    cache_keys = jnp.where(marks_key, own_cache, partner_cache)
    cache_values = jnp.where(marks_key, partner_cache, own_cache)
    scores = (
        jnp.einsum("thd,cd->thc", queries, cache_keys, preferred_element_type=jnp.float32)
        * score_scale
    )
    self_score = (
        jnp.sum(queries.astype(jnp.float32) * new_keys.astype(jnp.float32)[:, None, :], axis=-1)
        * score_scale
    )
    slot_index = jnp.arange(cache_keys.shape[0], dtype=jnp.int32)
    slot_group = slot_index // PROMPT_CAP
    slot_pos = slot_index % PROMPT_CAP
    visible = (
        (slot_group[None, :] == group_index[:, None])
        & (slot_pos[None, :] < row_length[:, None])
        & (slot_pos[None, :] > position[:, None] - WINDOW)
    )
    visible = visible[:, None, :]
    masked = jnp.where(visible, scores, -jnp.inf)
    ceiling = jnp.maximum(jnp.maximum(jnp.max(masked, axis=-1), self_score), sink_logit[None, :])
    weights = jnp.where(visible, jnp.exp(scores - ceiling[..., None]), 0.0)
    own_weight = jnp.exp(self_score - ceiling)
    denominator = jnp.sum(weights, axis=-1) + own_weight + jnp.exp(sink_logit[None, :] - ceiling)
    probabilities = (weights / denominator[..., None]).astype(jnp.bfloat16)
    own_prob = (own_weight / denominator).astype(jnp.bfloat16)
    context = jnp.einsum(
        "thc,cd->thd", probabilities, cache_values, preferred_element_type=jnp.float32
    )
    context = (
        context
        + own_prob.astype(jnp.float32)[..., None] * new_values.astype(jnp.float32)[:, None, :]
    )
    context = context.astype(jnp.bfloat16).reshape(tok_rows, local_heads * head_dim)
    places = slot_places(routes, copy_slot)
    return moe_call(
        context,
        out_weight,
        tokens,
        mixer_gain.reshape(1, width),
        places,
        places.T,
        route_weight,
        gate_weight[0],
        up_weight[0],
        down_weight[0],
        final_gain.reshape(1, -1),
    )


def solution(mesh):
    in_specs = (
        P("expert", None),
        P(),
        P(None, "tensor"),
        P("tensor", None, None),
        P("expert", "tensor", None, None),
        P("expert", None),
        P("expert"),
        P("expert"),
        P("tensor"),
        P("tensor", None),
        P(),
        P("expert", None),
        P("expert", None),
        P(),
        P("expert", None, "tensor"),
        P("expert", None, "tensor"),
        P("expert", "tensor", None),
        P("tensor"),
    )
    out_specs = P("expert", "tensor")
    return jax.shard_map(
        on_device, mesh=mesh, in_specs=in_specs, out_specs=out_specs, check_vma=False
    )
```

```python
import jax
import jax.numpy as jnp
from jax import lax
from jax.experimental import pallas as pl
from jax.experimental.pallas import tpu as pltpu
from jax.sharding import PartitionSpec as P

EXPERTS = 32
TOP = 4
PROMPT_CAP = 256
WINDOW = 192


EPSILON = 1e-06


def from_partner(block, axis, apart):
    count = lax.axis_size(axis)
    route = []
    for low in range(count):
        high = low | 1 << apart
        if high != low and high < count:
            route += [(low, high), (high, low)]
    return lax.ppermute(block, axis, route)


def rms_scale(values, gain_row):
    mean_square = jnp.mean(values * values, axis=-1, keepdims=True)
    return values * lax.rsqrt(mean_square + EPSILON) * gain_row.astype(jnp.float32)


def rotate(values, position):
    half_dim = values.shape[-1] // 2
    frequency = 10000.0 ** (-jnp.arange(half_dim, dtype=jnp.float32) / half_dim)
    angles = position.astype(jnp.float32)[:, None] * frequency[None, :]
    if values.ndim == 3:
        angles = angles[:, None, :]
    cosine_part = jnp.cos(angles)
    sine_part = jnp.sin(angles)
    front_half = values[..., :half_dim]
    back_half = values[..., half_dim:]
    return jnp.concatenate(
        [
            front_half * cosine_part - back_half * sine_part,
            front_half * sine_part + back_half * cosine_part,
        ],
        axis=-1,
    )


def slot_places(routes, copy_slot):
    rows = routes.shape[0]
    copies = copy_slot.shape[0]
    replicas = copies // EXPERTS
    block = jnp.arange(rows, dtype=jnp.int32) // (rows // replicas)
    row = jnp.arange(rows, dtype=jnp.int32)
    earlier = (block[:, None] == block[None, :]) & (row[None, :] < row[:, None])
    same = routes[:, :, None, None] == routes[None, None, :, :]
    rank = jnp.sum((same & earlier[:, None, :, None]).astype(jnp.int32), axis=(2, 3))
    wanted = routes * replicas + block[:, None]
    picks = wanted[:, :, None] == jnp.arange(copies, dtype=jnp.int32)
    holder = jnp.sum(jnp.where(picks, copy_slot, 0), axis=-1)
    return (holder % PLANE) * (2 * RING) + (holder // PLANE) * 2 + rank


RING = 16
PLANE = 8
LANES = 4
PART = 384
LAG = 3
MESH = pl.DeviceIdType.MESH


def far_first(t):
    half = (t + 1) // 2
    return RING // 2 + half * (1 - 2 * (t % 2))


def remote(src, dst, send, recv, expert, tensor):
    return pltpu.make_async_remote_copy(
        src_ref=src,
        dst_ref=dst,
        send_sem=send,
        recv_sem=recv,
        device_id=(expert, tensor),
        device_id_type=MESH,
    )


def dot(a, b):
    return jnp.dot(a, b, preferred_element_type=jnp.float32)


def dot_t(a, b):
    return lax.dot_general(a, b, (((1,), (1,)), ((), ())), preferred_element_type=jnp.float32)


def moe_kernel(
    context_ref,
    out_weight_ref,
    tokens_ref,
    mixer_ref,
    places_ref,
    places_t_ref,
    route_weight_ref,
    gate_ref,
    up_ref,
    down_ref,
    final_ref,
    out_ref,
    att,
    att_in,
    sq,
    sq_in,
    plane_out,
    plane_in,
    ring_out,
    box,
    partial,
    partial_in,
    joint,
    sums,
    sums_in,
    back_out,
    back_in,
    s_att,
    r_att,
    s_sq,
    r_sq,
    s_plane,
    r_plane,
    s_ring,
    r_ring,
    s_box,
    r_box,
    s_part,
    r_part,
    s_sum,
    r_sum,
    s_back,
    r_back,
):
    me = lax.axis_index("expert")
    x = lax.axis_index("tensor")
    z = me // PLANE
    yc = me % PLANE
    rows = tokens_ref.shape[0]
    width = LANES * PART

    barrier = pltpu.get_barrier_semaphore()

    def greet(expert, tensor):
        pl.semaphore_signal(barrier, inc=1, device_id=(expert, tensor), device_id_type=MESH)

    @pl.loop(1, RING)
    def _(d):
        greet((z + d) % RING * PLANE + yc, x)

    @pl.loop(1, PLANE)
    def _(d):
        greet(z * PLANE + (yc + d) % PLANE, x)

    @pl.loop(1, LANES)
    def _(d):
        greet(me, (x + d) % LANES)

    context = context_ref[...]
    for j in range(LANES):
        att[j] = dot(context, out_weight_ref[:, j * PART : (j + 1) * PART]).astype(jnp.bfloat16)
    pl.semaphore_wait(barrier, RING + PLANE + LANES - 3)

    def att_copy(d):
        to = (x + d) % LANES
        return remote(att.at[to], att_in.at[d - 1], s_att.at[d - 1], r_att.at[d - 1], me, to)

    for d in range(1, LANES):
        att_copy(d).start()
    mine = pl.ds(pl.multiple_of(x * PART, 128), PART)
    summed = att[x].astype(jnp.float32)
    for d in range(1, LANES):
        att_copy(d).wait_recv()
        summed = summed + att_in[d - 1].astype(jnp.float32)
    summed = summed.astype(jnp.bfloat16).astype(jnp.float32)
    residual = (tokens_ref[:, mine].astype(jnp.float32) + summed).astype(jnp.bfloat16)
    residual = residual.astype(jnp.float32)

    def whole_square(values, which):
        own = jnp.sum(values * values, axis=1, keepdims=True)
        sq[which] = jnp.broadcast_to(own, (rows, 128))

        def copy(d):
            to = (x + d) % LANES
            return remote(
                sq.at[which],
                sq_in.at[which, d - 1],
                s_sq.at[which, d - 1],
                r_sq.at[which, d - 1],
                me,
                to,
            )

        for d in range(1, LANES):
            copy(d).start()
        total = own
        for d in range(1, LANES):
            copy(d).wait_recv()
            total = total + sq_in[which, d - 1][:, :1]
        for d in range(1, LANES):
            copy(d).wait_send()
        return total

    total = whole_square(residual, 0)
    gain = mixer_ref[:, mine].astype(jnp.float32)
    mixed = (residual * lax.rsqrt(total / width + EPSILON) * gain).astype(jnp.bfloat16)

    slots = 2 * RING * PLANE
    place_row = lax.broadcasted_iota(jnp.int32, (slots, rows), 0)
    taken = jnp.zeros((slots, rows), jnp.float32)
    for k in range(TOP):
        taken = taken + (places_t_ref[k : k + 1, :] == place_row).astype(jnp.float32)
    outbox = dot(taken.astype(jnp.bfloat16), mixed).astype(jnp.bfloat16)
    plane_out[...] = outbox.reshape(PLANE, 2 * RING, PART)

    def plane_copy(d):
        to = (yc + d) % PLANE
        return remote(
            plane_out.at[to], plane_in.at[yc], s_plane.at[d], r_plane.at[d], z * PLANE + to, x
        )

    def plane_arrival(d):
        return remote(
            plane_out.at[yc],
            plane_in.at[(yc + PLANE - d) % PLANE],
            s_plane.at[d],
            r_plane.at[d],
            me,
            (x + 1) % LANES,
        )

    @pl.loop(1, PLANE)
    def _(d):
        plane_copy(d).start()

    plane_in[yc] = plane_out[yc]

    @pl.loop(1, PLANE)
    def _(d):
        plane_arrival(d).wait_recv()

    to_row = lax.broadcasted_iota(jnp.int32, (slots, slots), 0)
    from_row = lax.broadcasted_iota(jnp.int32, (slots, slots), 1)
    by_ring = ((to_row >> 1) & (PLANE - 1)) * (2 * RING) + (to_row >> 4) * 2 + (to_row & 1)
    by_ring = (by_ring == from_row).astype(jnp.float32).astype(jnp.bfloat16)
    by_plane = ((to_row >> 1) & (RING - 1)) * (2 * PLANE) + (to_row >> 5) * 2 + (to_row & 1)
    by_plane = (by_plane == from_row).astype(jnp.float32).astype(jnp.bfloat16)
    ordered = dot(by_ring, plane_in[...].reshape(slots, PART)).astype(jnp.bfloat16)
    ring_out[...] = ordered.reshape(RING, 2 * PLANE, PART)

    def ring_copy(d):
        to = (z + d) % RING
        return remote(
            ring_out.at[to], box.at[x, z], s_ring.at[d], r_ring.at[d], to * PLANE + yc, x
        )

    def ring_arrival(d):
        return remote(
            ring_out.at[z],
            box.at[x, (z + RING - d) % RING],
            s_ring.at[d],
            r_ring.at[d],
            me,
            (x + 1) % LANES,
        )

    def box_copy(d, j):
        at = (z + RING - d) % RING
        return remote(
            box.at[x, at],
            box.at[x, at],
            s_box.at[d, j - 1],
            r_box.at[d, j - 1],
            me,
            (x + j) % LANES,
        )

    def box_arrival(d, j):
        at = (z + RING - d) % RING
        return remote(
            box.at[x, at],
            box.at[(x + LANES - j) % LANES, at],
            s_box.at[d, j - 1],
            r_box.at[d, j - 1],
            me,
            (x + j) % LANES,
        )

    def relay_copy(d):
        at = (z + RING - d) % RING
        turn = d % 2
        lane = (x + LANES - 1 + 2 * turn) % LANES
        return remote(
            box.at[lane, at],
            box.at[lane, at],
            s_box.at[d, 1],
            r_box.at[d, 1],
            me,
            (x + 1 + 2 * turn) % LANES,
        )

    def relay(d):
        box_arrival(d, 1 + 2 * (d % 2)).wait_recv()
        relay_copy(d).start()

    @pl.loop(0, RING - 1)
    def _(t):
        ring_copy(far_first(t)).start()

    box[x, z] = ring_out[z]
    box_copy(0, 1).start()
    box_copy(0, 3).start()

    def pass_on(d):
        ring_arrival(d).wait_recv()
        box_copy(d, 1).start()
        box_copy(d, 3).start()

    pass_on(far_first(0))
    relay(0)

    @pl.loop(1, RING - 1)
    def _(t):
        pass_on(far_first(t))
        relay(far_first(t - 1))

    relay(far_first(RING - 2))

    @pl.loop(0, RING)
    def _(d):
        box_arrival(d, 3 - 2 * (d % 2)).wait_recv()
        box_arrival(d, 2).wait_recv()

    gate_val = jnp.zeros((slots, gate_ref.shape[0]), jnp.float32)
    up_val = jnp.zeros((slots, gate_ref.shape[0]), jnp.float32)
    for j in range(LANES):
        part = box[j].reshape(slots, PART)
        gate_val = gate_val + dot_t(part, gate_ref[:, j * PART : (j + 1) * PART])
        up_val = up_val + dot_t(part, up_ref[:, j * PART : (j + 1) * PART])
    hidden = (jnp.maximum(gate_val, 0.0) * up_val).astype(jnp.bfloat16)
    for j in range(LANES):
        product = dot(hidden, down_ref[:, j * PART : (j + 1) * PART]).astype(jnp.bfloat16)
        partial[j] = product.reshape(RING, 2 * PLANE, PART)

    def towards(d):
        return (x + 1 + 2 * (d % 2)) % LANES

    def away(d):
        return (x + LANES - 1 + 2 * (d % 2)) % LANES

    def near_copy(d):
        at, to = (z + d) % RING, towards(d)
        return remote(
            partial.at[to, at], partial_in.at[0, at], s_part.at[d, 0], r_part.at[d, 0], me, to
        )

    def far_copy(d):
        at, to = (z + d) % RING, (x + 2) % LANES
        return remote(
            partial.at[to, at], partial_in.at[1, at], s_part.at[d, 1], r_part.at[d, 1], me, away(d)
        )

    def joint_copy(d):
        at = (z + d) % RING
        return remote(
            joint.at[at], partial_in.at[2, at], s_part.at[d, 2], r_part.at[d, 2], me, away(d)
        )

    def sum_copy(d):
        to = (z + d) % RING
        return remote(sums.at[to], sums_in.at[z], s_sum.at[d], r_sum.at[d], to * PLANE + yc, x)

    def sum_arrival(d):
        return remote(
            sums.at[z],
            sums_in.at[(z + RING - d) % RING],
            s_sum.at[d],
            r_sum.at[d],
            me,
            (x + 1) % LANES,
        )

    @pl.loop(0, RING)
    def _(t):
        d = far_first(t)
        far_copy(d).start()
        near_copy(d).start()

    def join(d):
        at = (z + d) % RING
        far_copy(d).wait_recv()
        value = partial[away(d), at].astype(jnp.float32) + partial_in[1, at].astype(jnp.float32)
        joint[at] = value.astype(jnp.bfloat16)
        joint_copy(d).start()

    def add_parts(d):
        at = (z + d) % RING
        near_copy(d).wait_recv()
        joint_copy(d).wait_recv()
        value = partial[x, at].astype(jnp.float32) + partial_in[0, at].astype(jnp.float32)
        return (value + partial_in[2, at].astype(jnp.float32)).astype(jnp.bfloat16)

    for t in range(LAG):
        join(far_first(t))

    @pl.loop(0, RING - 1)
    def _(t):
        @pl.when(t + LAG < RING)
        def _():
            join(far_first(t + LAG))

        d = far_first(t)
        sums[(z + d) % RING] = add_parts(d)
        sum_copy(d).start()

    sums_in[z] = add_parts(0)

    @pl.loop(1, RING)
    def _(d):
        sum_arrival(d).wait_recv()

    ordered = dot(by_plane, sums_in[...].reshape(slots, PART)).astype(jnp.bfloat16)
    back_out[...] = ordered.reshape(PLANE, 2 * RING, PART)

    def back_copy(d):
        to = (yc + d) % PLANE
        return remote(
            back_out.at[to], back_in.at[yc], s_back.at[d], r_back.at[d], z * PLANE + to, x
        )

    def back_arrival(d):
        return remote(
            back_out.at[yc],
            back_in.at[(yc + PLANE - d) % PLANE],
            s_back.at[d],
            r_back.at[d],
            me,
            (x + 1) % LANES,
        )

    @pl.loop(1, PLANE)
    def _(d):
        back_copy(d).start()

    back_in[yc] = back_out[yc]
    place_col = lax.broadcasted_iota(jnp.int32, (rows, slots), 1)
    weigh = jnp.zeros((rows, slots), jnp.float32)
    for k in range(TOP):
        hit = places_ref[:, k : k + 1] == place_col
        weigh = weigh + jnp.where(hit, route_weight_ref[:, k : k + 1], 0.0)
    high = weigh.astype(jnp.bfloat16)
    low = (weigh - high.astype(jnp.float32)).astype(jnp.bfloat16)

    @pl.loop(1, PLANE)
    def _(d):
        back_arrival(d).wait_recv()

    returned = back_in[...].reshape(slots, PART)
    combined = residual + (dot(high, returned) + dot(low, returned))
    total = whole_square(combined, 1)
    final = final_ref[...].astype(jnp.float32)
    out_ref[...] = (combined * lax.rsqrt(total / width + EPSILON) * final).astype(out_ref.dtype)

    for d in range(1, LANES):
        att_copy(d).wait_send()

    @pl.loop(1, PLANE)
    def _(d):
        plane_copy(d).wait_send()
        back_copy(d).wait_send()

    @pl.loop(1, RING)
    def _(d):
        ring_copy(d).wait_send()
        sum_copy(d).wait_send()

    @pl.loop(0, RING)
    def _(d):
        box_copy(d, 1).wait_send()
        box_copy(d, 3).wait_send()
        relay_copy(d).wait_send()
        near_copy(d).wait_send()
        far_copy(d).wait_send()
        joint_copy(d).wait_send()


def moe_call(*operands):
    rows = operands[2].shape[0]
    vmem, sem = pltpu.VMEM, pltpu.SemaphoreType.DMA
    bf16 = jnp.bfloat16
    by_plane = vmem((PLANE, 2 * RING, PART), bf16)
    by_ring = vmem((RING, 2 * PLANE, PART), bf16)
    return pl.pallas_call(
        moe_kernel,
        out_shape=jax.ShapeDtypeStruct((rows, PART), bf16),
        in_specs=[pl.BlockSpec(memory_space=pltpu.VMEM)] * len(operands),
        out_specs=pl.BlockSpec(memory_space=pltpu.VMEM),
        scratch_shapes=[
            vmem((LANES, rows, PART), bf16),
            vmem((LANES - 1, rows, PART), bf16),
            vmem((2, rows, 128), jnp.float32),
            vmem((2, LANES - 1, rows, 128), jnp.float32),
            by_plane,
            by_plane,
            by_ring,
            vmem((LANES, RING, 2 * PLANE, PART), bf16),
            vmem((LANES, RING, 2 * PLANE, PART), bf16),
            vmem((LANES - 1, RING, 2 * PLANE, PART), bf16),
            by_ring,
            by_ring,
            by_ring,
            by_plane,
            by_plane,
        ]
        + [sem((LANES - 1,))] * 2
        + [sem((2, LANES - 1))] * 2
        + [sem((PLANE,))] * 2
        + [sem((RING,))] * 2
        + [sem((RING, LANES - 1))] * 4
        + [sem((RING,))] * 2
        + [sem((PLANE,))] * 2,
        compiler_params=pltpu.CompilerParams(collective_id=0, has_side_effects=True),
    )(*operands)


def on_device(
    tokens,
    attn_gain,
    query_weight,
    key_value_weight,
    paired_cache,
    prompt_length,
    group_index,
    offsets,
    sink_logit,
    out_weight,
    mixer_gain,
    routes,
    route_weight,
    copy_slot,
    gate_weight,
    up_weight,
    down_weight,
    final_gain,
):
    lanes = lax.axis_size("tensor")
    member = lax.axis_index("tensor")
    peers = lax.axis_size("expert")
    tok_rows, width = tokens.shape
    head_dim = key_value_weight.shape[2]
    local_heads = query_weight.shape[1] // head_dim
    score_scale = 1.0 / head_dim**0.5
    rows_f32 = tokens.astype(jnp.float32)
    normed_in = rms_scale(rows_f32, attn_gain).astype(jnp.bfloat16)
    lengths = prompt_length[0]
    prompt_slots = jnp.arange(lengths.shape[0], dtype=jnp.int32)
    row_length = jnp.sum(
        jnp.where(group_index[:, None] == prompt_slots[None, :], lengths[None, :], 0), axis=1
    )
    position = row_length + offsets
    queries = jnp.dot(normed_in, query_weight, preferred_element_type=jnp.float32).reshape(
        tok_rows, local_heads, head_dim
    )
    queries = rotate(queries, position).astype(jnp.bfloat16)
    projected = jnp.dot(normed_in, key_value_weight[0], preferred_element_type=jnp.float32)
    marks_key = member % 2 == 0
    own_projection = jnp.where(marks_key, rotate(projected, position), projected).astype(
        jnp.bfloat16
    )
    own_cache = paired_cache[0, 0]
    partner, partner_cache = from_partner((own_projection, own_cache), "tensor", 0)
    new_keys = jnp.where(marks_key, own_projection, partner)
    new_values = jnp.where(marks_key, partner, own_projection)
    cache_keys = jnp.where(marks_key, own_cache, partner_cache)
    cache_values = jnp.where(marks_key, partner_cache, own_cache)
    scores = (
        jnp.einsum("thd,cd->thc", queries, cache_keys, preferred_element_type=jnp.float32)
        * score_scale
    )
    self_score = (
        jnp.sum(queries.astype(jnp.float32) * new_keys.astype(jnp.float32)[:, None, :], axis=-1)
        * score_scale
    )
    slot_index = jnp.arange(cache_keys.shape[0], dtype=jnp.int32)
    slot_group = slot_index // PROMPT_CAP
    slot_pos = slot_index % PROMPT_CAP
    visible = (
        (slot_group[None, :] == group_index[:, None])
        & (slot_pos[None, :] < row_length[:, None])
        & (slot_pos[None, :] > position[:, None] - WINDOW)
    )
    visible = visible[:, None, :]
    masked = jnp.where(visible, scores, -jnp.inf)
    ceiling = jnp.maximum(jnp.maximum(jnp.max(masked, axis=-1), self_score), sink_logit[None, :])
    weights = jnp.where(visible, jnp.exp(scores - ceiling[..., None]), 0.0)
    own_weight = jnp.exp(self_score - ceiling)
    denominator = jnp.sum(weights, axis=-1) + own_weight + jnp.exp(sink_logit[None, :] - ceiling)
    probabilities = (weights / denominator[..., None]).astype(jnp.bfloat16)
    own_prob = (own_weight / denominator).astype(jnp.bfloat16)
    context = jnp.einsum(
        "thc,cd->thd", probabilities, cache_values, preferred_element_type=jnp.float32
    )
    context = (
        context
        + own_prob.astype(jnp.float32)[..., None] * new_values.astype(jnp.float32)[:, None, :]
    )
    context = context.astype(jnp.bfloat16).reshape(tok_rows, local_heads * head_dim)
    places = slot_places(routes, copy_slot)
    return moe_call(
        context,
        out_weight,
        tokens,
        mixer_gain.reshape(1, width),
        places,
        places.T,
        route_weight,
        gate_weight[0].T,
        up_weight[0].T,
        down_weight[0],
        final_gain.reshape(1, -1),
    )


def solution(mesh):
    in_specs = (
        P("expert", None),
        P(),
        P(None, "tensor"),
        P("tensor", None, None),
        P("expert", "tensor", None, None),
        P("expert", None),
        P("expert"),
        P("expert"),
        P("tensor"),
        P("tensor", None),
        P(),
        P("expert", None),
        P("expert", None),
        P(),
        P("expert", None, "tensor"),
        P("expert", None, "tensor"),
        P("expert", "tensor", None),
        P("tensor"),
    )
    out_specs = P("expert", "tensor")
    return jax.shard_map(
        on_device, mesh=mesh, in_specs=in_specs, out_specs=out_specs, check_vma=False
    )
```

```python
import jax
import jax.numpy as jnp
import numpy as np
from jax import lax
from jax.experimental import pallas as pl
from jax.experimental.pallas import tpu as pltpu
from jax.sharding import PartitionSpec as P

EXPERTS = 32
TOP = 4
PROMPT_CAP = 256
WINDOW = 192


EPSILON = 1e-06


def rms_scale(values, gain_row):
    mean_square = jnp.mean(values * values, axis=-1, keepdims=True)
    return values * lax.rsqrt(mean_square + EPSILON) * gain_row.astype(jnp.float32)


RING = 16
PLANE = 8
LANES = 4
PART = 384
HEAD = 128
HEADS = 3
CACHE = 768
MESH = pl.DeviceIdType.MESH


def far_first(t):
    half = (t + 1) // 2
    return RING // 2 + half * (1 - 2 * (t % 2))


def remote(src, dst, send, recv, expert, tensor):
    return pltpu.make_async_remote_copy(
        src_ref=src,
        dst_ref=dst,
        send_sem=send,
        recv_sem=recv,
        device_id=(expert, tensor),
        device_id_type=MESH,
    )


def dot(a, b):
    return jnp.dot(a, b, preferred_element_type=jnp.float32)


def dot_t(a, b):
    return lax.dot_general(a, b, (((1,), (1,)), ((), ())), preferred_element_type=jnp.float32)


def t_dot(a, b):
    return lax.dot_general(a, b, (((0,), (0,)), ((), ())), preferred_element_type=jnp.float32)


def layer_kernel(
    tokens_ref,
    attn_gain_ref,
    length_ref,
    group_ref,
    offset_ref,
    sink_ref,
    frequency_ref,
    mixer_ref,
    routes_ref,
    route_weight_ref,
    copy_slot_ref,
    final_ref,
    query_weight_hbm,
    kv_weight_hbm,
    cache_hbm,
    out_weight_hbm,
    gate_hbm,
    up_hbm,
    down_hbm,
    out_ref,
    query_weight,
    kv_weight,
    cache,
    out_weight,
    gate,
    up,
    down,
    new_kv,
    att,
    att_in,
    sq,
    sq_in,
    plane_out,
    plane_in,
    ring_out,
    box,
    partial,
    partial_in,
    sums,
    sums_in,
    back_out,
    back_in,
    s_att,
    r_att,
    s_sq,
    r_sq,
    s_plane,
    r_plane,
    s_ring,
    r_ring,
    s_box,
    r_box,
    s_part,
    r_part,
    s_sum,
    r_sum,
    s_back,
    r_back,
    s_kv,
    r_kv,
    s_load,
):
    me = lax.axis_index("expert")
    x = lax.axis_index("tensor")
    z = me // PLANE
    yc = me % PLANE
    rows = tokens_ref.shape[0]
    width = LANES * PART

    barrier = pltpu.get_barrier_semaphore()

    def greet(expert, tensor):
        pl.semaphore_signal(barrier, inc=1, device_id=(expert, tensor), device_id_type=MESH)

    @pl.loop(1, RING)
    def _(d):
        greet((z + d) % RING * PLANE + yc, x)

    @pl.loop(1, PLANE)
    def _(d):
        greet(z * PLANE + (yc + d) % PLANE, x)

    @pl.loop(1, LANES)
    def _(d):
        greet(me, (x + d) % LANES)

    half = x % 2
    loads = [
        pltpu.make_async_copy(src, dst, s_load.at[i])
        for i, (src, dst) in enumerate(
            [
                (query_weight_hbm, query_weight),
                (kv_weight_hbm, kv_weight),
                (cache_hbm, cache.at[half]),
                (out_weight_hbm, out_weight),
                (gate_hbm, gate),
                (up_hbm, up),
                (down_hbm, down),
            ]
        )
    ]
    for load in loads:
        load.start()

    slots = 2 * RING * PLANE
    copies = copy_slot_ref.shape[1]
    replicas = copies // EXPERTS
    group_rows = rows // replicas
    early = lax.broadcasted_iota(jnp.int32, (rows, rows), 0)
    late = lax.broadcasted_iota(jnp.int32, (rows, rows), 1)
    before = (early // group_rows == late // group_rows) & (early < late)
    before = before.astype(jnp.float32).astype(jnp.bfloat16)
    expert_row = lax.broadcasted_iota(jnp.int32, (EXPERTS, rows), 0)
    named = [
        (routes_ref[k : k + 1, :] == expert_row).astype(jnp.float32) for k in range(TOP)
    ]
    earlier = dot(sum(named).astype(jnp.bfloat16), before)
    copy_row = lax.broadcasted_iota(jnp.int32, (copies, rows), 0)
    row_block = lax.broadcasted_iota(jnp.int32, (1, rows), 1) // group_rows
    slot_of = jnp.broadcast_to(copy_slot_ref[...].astype(jnp.float32), (16, copies))
    slot_of = slot_of.astype(jnp.bfloat16)
    place_row = lax.broadcasted_iota(jnp.int32, (slots, rows), 0)
    taken = jnp.zeros((slots, rows), jnp.float32)
    weigh = jnp.zeros((slots, rows), jnp.float32)
    for k in range(TOP):
        rank = jnp.sum(named[k] * earlier, axis=0, keepdims=True).astype(jnp.int32)
        wanted = routes_ref[k : k + 1, :] * replicas + row_block
        picks = (wanted == copy_row).astype(jnp.float32).astype(jnp.bfloat16)
        holder = dot(slot_of, picks)[:1].astype(jnp.int32)
        place = (holder & (PLANE - 1)) * (2 * RING) + (holder >> 3) * 2 + rank
        hit = place == place_row
        taken = taken + hit.astype(jnp.float32)
        weigh = weigh + jnp.where(hit, route_weight_ref[k : k + 1, :], 0.0)

    values = tokens_ref[...].astype(jnp.float32)
    normed_in = rms_scale(values, attn_gain_ref[...]).astype(jnp.bfloat16)

    def column(row):
        return jnp.sum(jnp.where(early == late, row.astype(jnp.float32), 0.0), axis=1, keepdims=True)

    group = column(group_ref[...])
    row_length = jnp.zeros((rows, 1), jnp.float32)
    for p in range(length_ref.shape[1]):
        this = length_ref[:, p : p + 1].astype(jnp.float32)
        row_length = row_length + jnp.where(group == p, this, 0.0)
    position = row_length + column(offset_ref[...])
    angles = position * frequency_ref[...]
    lane = lax.broadcasted_iota(jnp.int32, angles.shape, 1)
    cosine = jnp.cos(angles)
    sine = jnp.where(lane < HEAD // 2, -jnp.sin(angles), jnp.sin(angles))
    loads[0].wait()
    loads[1].wait()
    queries = dot(normed_in, query_weight[...])
    heads = []
    for h in range(HEADS):
        one = queries[:, h * HEAD : (h + 1) * HEAD]
        heads.append(one * cosine + pltpu.roll(one, HEAD // 2, 1) * sine)
    queries = jnp.concatenate(heads, axis=0).astype(jnp.bfloat16)
    projected = dot(normed_in, kv_weight[...])
    turned = projected * cosine + pltpu.roll(projected, HEAD // 2, 1) * sine
    marks_key = lane * 0 + half == 0
    new_kv[half] = jnp.where(marks_key, turned, projected).astype(jnp.bfloat16)
    loads[2].wait()
    pl.semaphore_wait(barrier, RING + PLANE + LANES - 3)

    partner = x + 1 - 2 * half
    new_copy = remote(
        new_kv.at[half], new_kv.at[half], s_kv.at[0], r_kv.at[0], me, partner
    )
    cache_copy = remote(cache.at[half], cache.at[half], s_kv.at[1], r_kv.at[1], me, partner)
    new_arrival = remote(
        new_kv.at[half], new_kv.at[1 - half], s_kv.at[0], r_kv.at[0], me, partner
    )
    cache_arrival = remote(
        cache.at[half], cache.at[1 - half], s_kv.at[1], r_kv.at[1], me, partner
    )
    new_copy.start()
    cache_copy.start()

    def stacked(block):
        return jnp.concatenate([block] * HEADS, axis=0)

    total_rows = HEADS * rows
    scale = HEAD**-0.5
    slot = lax.broadcasted_iota(jnp.int32, (rows, CACHE), 1)
    slot_pos = (slot & (PROMPT_CAP - 1)).astype(jnp.float32)
    visible = (
        ((slot >> 8).astype(jnp.float32) == group)
        & (slot_pos < row_length)
        & (slot_pos > position - WINDOW)
    )
    visible = stacked(jnp.where(visible, 1.0, 0.0)) > 0.5
    sinks = jnp.concatenate(
        [jnp.broadcast_to(sink_ref[:, h : h + 1], (rows, 1)) for h in range(HEADS)], axis=0
    )
    new_arrival.wait_recv()
    new_key = stacked(new_kv[0].astype(jnp.float32))
    new_value = stacked(new_kv[1].astype(jnp.float32))
    self_score = jnp.sum(queries.astype(jnp.float32) * new_key, axis=1, keepdims=True) * scale
    cache_arrival.wait_recv()
    scores = dot_t(queries, cache[0]) * scale
    ceiling = jnp.max(jnp.where(visible, scores, -jnp.inf), axis=1, keepdims=True)
    ceiling = jnp.maximum(jnp.maximum(ceiling, self_score), sinks)
    weights = jnp.where(visible, jnp.exp(scores - ceiling), 0.0)
    own_weight = jnp.exp(self_score - ceiling)
    denominator = (
        jnp.sum(weights, axis=1, keepdims=True) + own_weight + jnp.exp(sinks - ceiling)
    )
    probabilities = (weights / denominator).astype(jnp.bfloat16)
    own_prob = (own_weight / denominator).astype(jnp.bfloat16).astype(jnp.float32)
    context = dot(probabilities, cache[1]) + own_prob * new_value
    context = context.astype(jnp.bfloat16)
    context = jnp.concatenate(
        [context[h * rows : (h + 1) * rows] for h in range(HEADS)], axis=1
    )
    loads[3].wait()

    for j in range(LANES):
        att[j] = dot(context, out_weight[:, j * PART : (j + 1) * PART]).astype(jnp.bfloat16)

    def att_copy(d):
        to = (x + d) % LANES
        return remote(att.at[to], att_in.at[d - 1], s_att.at[d - 1], r_att.at[d - 1], me, to)

    for d in range(1, LANES):
        att_copy(d).start()
    mine = pl.ds(pl.multiple_of(x * PART, 128), PART)
    summed = att[x].astype(jnp.float32)
    for d in range(1, LANES):
        att_copy(d).wait_recv()
        summed = summed + att_in[d - 1].astype(jnp.float32)
    summed = summed.astype(jnp.bfloat16).astype(jnp.float32)
    residual = (tokens_ref[:, mine].astype(jnp.float32) + summed).astype(jnp.bfloat16)
    residual = residual.astype(jnp.float32)

    def whole_square(values, which):
        own = jnp.sum(values * values, axis=1, keepdims=True)
        sq[which] = jnp.broadcast_to(own, (rows, 128))

        def copy(d):
            to = (x + d) % LANES
            return remote(
                sq.at[which],
                sq_in.at[which, d - 1],
                s_sq.at[which, d - 1],
                r_sq.at[which, d - 1],
                me,
                to,
            )

        for d in range(1, LANES):
            copy(d).start()
        total = own
        for d in range(1, LANES):
            copy(d).wait_recv()
            total = total + sq_in[which, d - 1][:, :1]
        for d in range(1, LANES):
            copy(d).wait_send()
        return total

    total = whole_square(residual, 0)
    gain = mixer_ref[:, mine].astype(jnp.float32)
    mixed = (residual * lax.rsqrt(total / width + EPSILON) * gain).astype(jnp.bfloat16)

    outbox = dot(taken.astype(jnp.bfloat16), mixed).astype(jnp.bfloat16)
    plane_out[...] = outbox.reshape(PLANE, 2 * RING, PART)

    def plane_copy(d):
        to = (yc + d) % PLANE
        return remote(
            plane_out.at[to], plane_in.at[yc], s_plane.at[d], r_plane.at[d], z * PLANE + to, x
        )

    def plane_arrival(d):
        return remote(
            plane_out.at[yc],
            plane_in.at[(yc + PLANE - d) % PLANE],
            s_plane.at[d],
            r_plane.at[d],
            me,
            (x + 1) % LANES,
        )

    @pl.loop(1, PLANE)
    def _(d):
        plane_copy(d).start()

    plane_in[yc] = plane_out[yc]

    @pl.loop(1, PLANE)
    def _(d):
        plane_arrival(d).wait_recv()

    to_row = lax.broadcasted_iota(jnp.int32, (slots, slots), 0)
    from_row = lax.broadcasted_iota(jnp.int32, (slots, slots), 1)
    by_ring = ((to_row >> 1) & (PLANE - 1)) * (2 * RING) + (to_row >> 4) * 2 + (to_row & 1)
    by_ring = (by_ring == from_row).astype(jnp.float32).astype(jnp.bfloat16)
    by_plane = ((to_row >> 1) & (RING - 1)) * (2 * PLANE) + (to_row >> 5) * 2 + (to_row & 1)
    by_plane = (by_plane == from_row).astype(jnp.float32).astype(jnp.bfloat16)
    ordered = dot(by_ring, plane_in[...].reshape(slots, PART)).astype(jnp.bfloat16)
    ring_out[...] = ordered.reshape(RING, 2 * PLANE, PART)

    def ring_copy(d):
        to = (z + d) % RING
        return remote(
            ring_out.at[to], box.at[x, z], s_ring.at[d], r_ring.at[d], to * PLANE + yc, x
        )

    def ring_arrival(d):
        return remote(
            ring_out.at[z],
            box.at[x, (z + RING - d) % RING],
            s_ring.at[d],
            r_ring.at[d],
            me,
            (x + 1) % LANES,
        )

    def box_copy(d, j):
        at = (z + RING - d) % RING
        return remote(
            box.at[x, at],
            box.at[x, at],
            s_box.at[d, j - 1],
            r_box.at[d, j - 1],
            me,
            (x + j) % LANES,
        )

    def box_arrival(d, j):
        at = (z + RING - d) % RING
        return remote(
            box.at[x, at],
            box.at[(x + LANES - j) % LANES, at],
            s_box.at[d, j - 1],
            r_box.at[d, j - 1],
            me,
            (x + j) % LANES,
        )

    @pl.loop(0, RING - 1)
    def _(t):
        ring_copy(far_first(t)).start()

    box[x, z] = ring_out[z]
    for j in range(1, LANES):
        box_copy(0, j).start()

    @pl.loop(0, RING - 1)
    def _(t):
        d = far_first(t)
        ring_arrival(d).wait_recv()
        for j in range(1, LANES):
            box_copy(d, j).start()

    @pl.loop(0, RING)
    def _(d):
        for j in range(1, LANES):
            box_arrival(d, j).wait_recv()

    for load in loads[4:]:
        load.wait()
    gate_val = jnp.zeros((slots, gate.shape[0]), jnp.float32)
    up_val = jnp.zeros((slots, gate.shape[0]), jnp.float32)
    for j in range(LANES):
        part = box[j].reshape(slots, PART)
        gate_val = gate_val + dot_t(part, gate[:, j * PART : (j + 1) * PART])
        up_val = up_val + dot_t(part, up[:, j * PART : (j + 1) * PART])
    hidden = (jnp.maximum(gate_val, 0.0) * up_val).astype(jnp.bfloat16)
    for j in range(LANES):
        product = dot(hidden, down[:, j * PART : (j + 1) * PART]).astype(jnp.bfloat16)
        partial[j] = product.reshape(RING, 2 * PLANE, PART)

    def part_copy(d, j):
        at = (z + d) % RING
        to = (x + j) % LANES
        return remote(
            partial.at[to, at],
            partial_in.at[j - 1, at],
            s_part.at[d, j - 1],
            r_part.at[d, j - 1],
            me,
            to,
        )

    def sum_copy(d):
        to = (z + d) % RING
        return remote(sums.at[to], sums_in.at[z], s_sum.at[d], r_sum.at[d], to * PLANE + yc, x)

    def sum_arrival(d):
        return remote(
            sums.at[z],
            sums_in.at[(z + RING - d) % RING],
            s_sum.at[d],
            r_sum.at[d],
            me,
            (x + 1) % LANES,
        )

    @pl.loop(0, RING)
    def _(t):
        for j in range(1, LANES):
            part_copy(far_first(t), j).start()

    def add_parts(d):
        at = (z + d) % RING
        value = partial[x, at].astype(jnp.float32)
        for j in range(1, LANES):
            part_copy(d, j).wait_recv()
            value = value + partial_in[j - 1, at].astype(jnp.float32)
        return value.astype(jnp.bfloat16)

    @pl.loop(0, RING - 1)
    def _(t):
        d = far_first(t)
        sums[(z + d) % RING] = add_parts(d)
        sum_copy(d).start()

    sums_in[z] = add_parts(0)

    @pl.loop(1, RING)
    def _(d):
        sum_arrival(d).wait_recv()

    ordered = dot(by_plane, sums_in[...].reshape(slots, PART)).astype(jnp.bfloat16)
    back_out[...] = ordered.reshape(PLANE, 2 * RING, PART)

    def back_copy(d):
        to = (yc + d) % PLANE
        return remote(
            back_out.at[to], back_in.at[yc], s_back.at[d], r_back.at[d], z * PLANE + to, x
        )

    def back_arrival(d):
        return remote(
            back_out.at[yc],
            back_in.at[(yc + PLANE - d) % PLANE],
            s_back.at[d],
            r_back.at[d],
            me,
            (x + 1) % LANES,
        )

    @pl.loop(1, PLANE)
    def _(d):
        back_copy(d).start()

    back_in[yc] = back_out[yc]
    high = weigh.astype(jnp.bfloat16)
    low = (weigh - high.astype(jnp.float32)).astype(jnp.bfloat16)

    @pl.loop(1, PLANE)
    def _(d):
        back_arrival(d).wait_recv()

    returned = back_in[...].reshape(slots, PART)
    combined = residual + (t_dot(high, returned) + t_dot(low, returned))
    total = whole_square(combined, 1)
    final = final_ref[...].astype(jnp.float32)
    out_ref[...] = (combined * lax.rsqrt(total / width + EPSILON) * final).astype(out_ref.dtype)

    new_copy.wait_send()
    cache_copy.wait_send()
    for d in range(1, LANES):
        att_copy(d).wait_send()

    @pl.loop(1, PLANE)
    def _(d):
        plane_copy(d).wait_send()
        back_copy(d).wait_send()

    @pl.loop(1, RING)
    def _(d):
        ring_copy(d).wait_send()
        sum_copy(d).wait_send()

    @pl.loop(0, RING)
    def _(d):
        for j in range(1, LANES):
            box_copy(d, j).wait_send()
            part_copy(d, j).wait_send()


def layer_call(small, large):
    rows = small[0].shape[0]
    vmem, sem = pltpu.VMEM, pltpu.SemaphoreType.DMA
    bf16 = jnp.bfloat16
    by_plane = vmem((PLANE, 2 * RING, PART), bf16)
    by_ring = vmem((RING, 2 * PLANE, PART), bf16)
    held = [vmem(block.shape, bf16) for block in large]
    held[2] = vmem((2, CACHE, HEAD), bf16)
    return pl.pallas_call(
        layer_kernel,
        out_shape=jax.ShapeDtypeStruct((rows, PART), bf16),
        in_specs=[pl.BlockSpec(memory_space=pltpu.VMEM)] * len(small)
        + [pl.BlockSpec(memory_space=pl.ANY)] * len(large),
        out_specs=pl.BlockSpec(memory_space=pltpu.VMEM),
        scratch_shapes=held
        + [
            vmem((2, rows, HEAD), bf16),
            vmem((LANES, rows, PART), bf16),
            vmem((LANES - 1, rows, PART), bf16),
            vmem((2, rows, 128), jnp.float32),
            vmem((2, LANES - 1, rows, 128), jnp.float32),
            by_plane,
            by_plane,
            by_ring,
            vmem((LANES, RING, 2 * PLANE, PART), bf16),
            vmem((LANES, RING, 2 * PLANE, PART), bf16),
            vmem((LANES - 1, RING, 2 * PLANE, PART), bf16),
            by_ring,
            by_ring,
            by_plane,
            by_plane,
        ]
        + [sem((LANES - 1,))] * 2
        + [sem((2, LANES - 1))] * 2
        + [sem((PLANE,))] * 2
        + [sem((RING,))] * 2
        + [sem((RING, LANES - 1))] * 4
        + [sem((RING,))] * 2
        + [sem((PLANE,))] * 2
        + [sem((2,))] * 2
        + [sem((7,))],
        compiler_params=pltpu.CompilerParams(collective_id=0, has_side_effects=True),
    )(*small, *large)


def on_device(
    tokens,
    attn_gain,
    query_weight,
    key_value_weight,
    paired_cache,
    prompt_length,
    group_index,
    offsets,
    sink_logit,
    out_weight,
    mixer_gain,
    routes,
    route_weight,
    copy_slot,
    gate_weight,
    up_weight,
    down_weight,
    final_gain,
):
    half = HEAD // 2
    frequency = 10000.0 ** (-np.arange(half, dtype=np.float64) / half)
    frequency = jnp.asarray(np.tile(frequency, 2)[None, :], jnp.float32)
    small = [
        tokens,
        attn_gain.reshape(1, -1),
        prompt_length,
        group_index.reshape(1, -1),
        offsets.reshape(1, -1),
        sink_logit.reshape(1, -1),
        frequency,
        mixer_gain.reshape(1, -1),
        routes.T,
        route_weight.T,
        copy_slot.reshape(1, -1),
        final_gain.reshape(1, -1),
    ]
    large = [
        query_weight,
        key_value_weight[0],
        paired_cache[0, 0],
        out_weight,
        gate_weight[0].T,
        up_weight[0].T,
        down_weight[0],
    ]
    return layer_call(small, large)


def solution(mesh):
    in_specs = (
        P("expert", None),
        P(),
        P(None, "tensor"),
        P("tensor", None, None),
        P("expert", "tensor", None, None),
        P("expert", None),
        P("expert"),
        P("expert"),
        P("tensor"),
        P("tensor", None),
        P(),
        P("expert", None),
        P("expert", None),
        P(),
        P("expert", None, "tensor"),
        P("expert", None, "tensor"),
        P("expert", "tensor", None),
        P("tensor"),
    )
    out_specs = P("expert", "tensor")
    return jax.shard_map(
        on_device, mesh=mesh, in_specs=in_specs, out_specs=out_specs, check_vma=False
    )
```

```python
import jax
import jax.numpy as jnp
import numpy as np
from jax import lax
from jax.experimental import pallas as pl
from jax.experimental.pallas import tpu as pltpu
from jax.sharding import PartitionSpec as P

EXPERTS = 32
TOP = 4
PROMPT_CAP = 256
WINDOW = 192


EPSILON = 1e-06


def rms_scale(values, gain_row):
    mean_square = jnp.mean(values * values, axis=-1, keepdims=True)
    return values * lax.rsqrt(mean_square + EPSILON) * gain_row.astype(jnp.float32)


RING = 16
PLANE = 8
LANES = 4
PART = 384
HEAD = 128
HEADS = 3
CACHE = 768
MESH = pl.DeviceIdType.MESH


def far_first(t):
    half = (t + 1) // 2
    return RING // 2 + half * (1 - 2 * (t % 2))


def remote(src, dst, send, recv, expert, tensor):
    return pltpu.make_async_remote_copy(
        src_ref=src,
        dst_ref=dst,
        send_sem=send,
        recv_sem=recv,
        device_id=(expert, tensor),
        device_id_type=MESH,
    )


def dot(a, b):
    return jnp.dot(a, b, preferred_element_type=jnp.float32)


def dot_t(a, b):
    return lax.dot_general(a, b, (((1,), (1,)), ((), ())), preferred_element_type=jnp.float32)


def as_row(values):
    return values.astype(jnp.float32).reshape(1, -1)


def t_dot(a, b):
    return lax.dot_general(a, b, (((0,), (0,)), ((), ())), preferred_element_type=jnp.float32)


def layer_kernel(
    tokens_ref,
    attn_gain_ref,
    length_ref,
    group_ref,
    offset_ref,
    sink_ref,
    frequency_ref,
    mixer_ref,
    routes_ref,
    route_weight_ref,
    copy_slot_ref,
    final_ref,
    query_weight_hbm,
    kv_weight_hbm,
    cache_hbm,
    out_weight_hbm,
    gate_hbm,
    up_hbm,
    down_hbm,
    out_ref,
    query_weight,
    kv_weight,
    cache,
    out_weight,
    gate,
    up,
    down,
    new_kv,
    att,
    att_in,
    sq,
    sq_in,
    plane_out,
    plane_in,
    ring_out,
    box,
    partial,
    partial_in,
    sums,
    sums_in,
    back_out,
    back_in,
    s_att,
    r_att,
    s_sq,
    r_sq,
    s_plane,
    r_plane,
    s_ring,
    r_ring,
    s_box,
    r_box,
    s_part,
    r_part,
    s_sum,
    r_sum,
    s_back,
    r_back,
    s_kv,
    r_kv,
    s_load,
):
    me = lax.axis_index("expert")
    x = lax.axis_index("tensor")
    z = me // PLANE
    yc = me % PLANE
    rows = tokens_ref.shape[0]
    width = LANES * PART

    barrier = pltpu.get_barrier_semaphore()

    def greet(expert, tensor):
        pl.semaphore_signal(barrier, inc=1, device_id=(expert, tensor), device_id_type=MESH)

    @pl.loop(1, RING)
    def _(d):
        greet((z + d) % RING * PLANE + yc, x)

    @pl.loop(1, PLANE)
    def _(d):
        greet(z * PLANE + (yc + d) % PLANE, x)

    @pl.loop(1, LANES)
    def _(d):
        greet(me, (x + d) % LANES)

    half = x % 2
    loads = [
        pltpu.make_async_copy(src, dst, s_load.at[i])
        for i, (src, dst) in enumerate(
            [
                (query_weight_hbm, query_weight),
                (kv_weight_hbm, kv_weight),
                (cache_hbm, cache.at[half]),
                (out_weight_hbm, out_weight),
                (gate_hbm, gate),
                (up_hbm, up),
                (down_hbm, down),
            ]
        )
    ]
    for load in loads:
        load.start()

    slots = 2 * RING * PLANE
    copies = copy_slot_ref.shape[1]
    replicas = copies // EXPERTS
    group_rows = rows // replicas
    early = lax.broadcasted_iota(jnp.int32, (rows, rows), 0)
    late = lax.broadcasted_iota(jnp.int32, (rows, rows), 1)
    before = (early // group_rows == late // group_rows) & (early < late)
    before = before.astype(jnp.float32).astype(jnp.bfloat16)
    expert_row = lax.broadcasted_iota(jnp.int32, (EXPERTS, rows), 0)
    named = [
        (routes_ref[k : k + 1, :] == expert_row).astype(jnp.float32) for k in range(TOP)
    ]
    earlier = dot(sum(named).astype(jnp.bfloat16), before)
    copy_row = lax.broadcasted_iota(jnp.int32, (copies, rows), 0)
    row_block = lax.broadcasted_iota(jnp.int32, (1, rows), 1) // group_rows
    slot_of = jnp.broadcast_to(copy_slot_ref[...].astype(jnp.float32), (16, copies))
    slot_of = slot_of.astype(jnp.bfloat16)
    place_row = lax.broadcasted_iota(jnp.int32, (slots, rows), 0)
    taken = jnp.zeros((slots, rows), jnp.float32)
    weigh = jnp.zeros((slots, rows), jnp.float32)
    for k in range(TOP):
        rank = jnp.sum(named[k] * earlier, axis=0, keepdims=True).astype(jnp.int32)
        wanted = routes_ref[k : k + 1, :] * replicas + row_block
        picks = (wanted == copy_row).astype(jnp.float32).astype(jnp.bfloat16)
        holder = dot(slot_of, picks)[:1].astype(jnp.int32)
        place = (holder & (PLANE - 1)) * (2 * RING) + (holder >> 3) * 2 + rank
        hit = place == place_row
        taken = taken + hit.astype(jnp.float32)
        weigh = weigh + jnp.where(hit, route_weight_ref[k : k + 1, :], 0.0)

    values = tokens_ref[...].astype(jnp.float32)
    normed_in = rms_scale(values, as_row(attn_gain_ref[...])).astype(jnp.bfloat16)

    def column(row):
        return jnp.sum(jnp.where(early == late, row.astype(jnp.float32), 0.0), axis=1, keepdims=True)

    group = column(group_ref[...])
    row_length = jnp.zeros((rows, 1), jnp.float32)
    for p in range(length_ref.shape[1]):
        this = length_ref[:, p : p + 1].astype(jnp.float32)
        row_length = row_length + jnp.where(group == p, this, 0.0)
    position = row_length + column(offset_ref[...])
    angles = position * frequency_ref[...]
    lane = lax.broadcasted_iota(jnp.int32, angles.shape, 1)
    cosine = jnp.cos(angles)
    sine = jnp.where(lane < HEAD // 2, -jnp.sin(angles), jnp.sin(angles))
    loads[0].wait()
    loads[1].wait()
    queries = dot(normed_in, query_weight[...])
    heads = []
    for h in range(HEADS):
        one = queries[:, h * HEAD : (h + 1) * HEAD]
        heads.append(one * cosine + pltpu.roll(one, HEAD // 2, 1) * sine)
    queries = jnp.concatenate(heads, axis=0).astype(jnp.bfloat16)
    projected = dot(normed_in, kv_weight[...])
    turned = projected * cosine + pltpu.roll(projected, HEAD // 2, 1) * sine
    marks_key = lane * 0 + half == 0
    new_kv[half] = jnp.where(marks_key, turned, projected).astype(jnp.bfloat16)
    loads[2].wait()
    pl.semaphore_wait(barrier, RING + PLANE + LANES - 3)

    partner = x + 1 - 2 * half
    new_copy = remote(
        new_kv.at[half], new_kv.at[half], s_kv.at[0], r_kv.at[0], me, partner
    )
    cache_copy = remote(cache.at[half], cache.at[half], s_kv.at[1], r_kv.at[1], me, partner)
    new_arrival = remote(
        new_kv.at[half], new_kv.at[1 - half], s_kv.at[0], r_kv.at[0], me, partner
    )
    cache_arrival = remote(
        cache.at[half], cache.at[1 - half], s_kv.at[1], r_kv.at[1], me, partner
    )
    new_copy.start()
    cache_copy.start()

    def stacked(block):
        return jnp.concatenate([block] * HEADS, axis=0)

    total_rows = HEADS * rows
    scale = HEAD**-0.5
    slot = lax.broadcasted_iota(jnp.int32, (rows, CACHE), 1)
    slot_pos = (slot & (PROMPT_CAP - 1)).astype(jnp.float32)
    visible = (
        ((slot >> 8).astype(jnp.float32) == group)
        & (slot_pos < row_length)
        & (slot_pos > position - WINDOW)
    )
    visible = stacked(jnp.where(visible, 1.0, 0.0)) > 0.5
    sinks = jnp.concatenate(
        [jnp.broadcast_to(sink_ref[:, h : h + 1], (rows, 1)) for h in range(HEADS)], axis=0
    )
    new_arrival.wait_recv()
    new_key = stacked(new_kv[0].astype(jnp.float32))
    new_value = stacked(new_kv[1].astype(jnp.float32))
    self_score = jnp.sum(queries.astype(jnp.float32) * new_key, axis=1, keepdims=True) * scale
    cache_arrival.wait_recv()
    scores = dot_t(queries, cache[0]) * scale
    ceiling = jnp.max(jnp.where(visible, scores, -jnp.inf), axis=1, keepdims=True)
    ceiling = jnp.maximum(jnp.maximum(ceiling, self_score), sinks)
    weights = jnp.where(visible, jnp.exp(scores - ceiling), 0.0)
    own_weight = jnp.exp(self_score - ceiling)
    denominator = (
        jnp.sum(weights, axis=1, keepdims=True) + own_weight + jnp.exp(sinks - ceiling)
    )
    probabilities = (weights / denominator).astype(jnp.bfloat16)
    own_prob = (own_weight / denominator).astype(jnp.bfloat16).astype(jnp.float32)
    context = dot(probabilities, cache[1]) + own_prob * new_value
    context = context.astype(jnp.bfloat16)
    context = jnp.concatenate(
        [context[h * rows : (h + 1) * rows] for h in range(HEADS)], axis=1
    )
    loads[3].wait()

    for j in range(LANES):
        att[j] = dot(context, out_weight[:, j * PART : (j + 1) * PART]).astype(jnp.bfloat16)

    def att_copy(d):
        to = (x + d) % LANES
        return remote(att.at[to], att_in.at[d - 1], s_att.at[d - 1], r_att.at[d - 1], me, to)

    for d in range(1, LANES):
        att_copy(d).start()
    mine = pl.ds(pl.multiple_of(x * PART, 128), PART)
    summed = att[x].astype(jnp.float32)
    for d in range(1, LANES):
        att_copy(d).wait_recv()
        summed = summed + att_in[d - 1].astype(jnp.float32)
    summed = summed.astype(jnp.bfloat16).astype(jnp.float32)
    residual = (tokens_ref[:, mine].astype(jnp.float32) + summed).astype(jnp.bfloat16)
    residual = residual.astype(jnp.float32)

    def whole_square(values, which):
        own = jnp.sum(values * values, axis=1, keepdims=True)
        sq[which] = jnp.broadcast_to(own, (rows, 128))

        def copy(d):
            to = (x + d) % LANES
            return remote(
                sq.at[which],
                sq_in.at[which, d - 1],
                s_sq.at[which, d - 1],
                r_sq.at[which, d - 1],
                me,
                to,
            )

        for d in range(1, LANES):
            copy(d).start()
        total = own
        for d in range(1, LANES):
            copy(d).wait_recv()
            total = total + sq_in[which, d - 1][:, :1]
        for d in range(1, LANES):
            copy(d).wait_send()
        return total

    total = whole_square(residual, 0)
    gains = as_row(mixer_ref[...])
    gain = jnp.zeros((1, PART), jnp.float32)
    for j in range(LANES):
        this = (x == j).astype(jnp.float32)
        gain = gain + this * gains[:, j * PART : (j + 1) * PART]
    mixed = (residual * lax.rsqrt(total / width + EPSILON) * gain).astype(jnp.bfloat16)

    outbox = dot(taken.astype(jnp.bfloat16), mixed).astype(jnp.bfloat16)
    plane_out[...] = outbox.reshape(PLANE, 2 * RING, PART)

    def plane_copy(d):
        to = (yc + d) % PLANE
        return remote(
            plane_out.at[to], plane_in.at[yc], s_plane.at[d], r_plane.at[d], z * PLANE + to, x
        )

    def plane_arrival(d):
        return remote(
            plane_out.at[yc],
            plane_in.at[(yc + PLANE - d) % PLANE],
            s_plane.at[d],
            r_plane.at[d],
            me,
            (x + 1) % LANES,
        )

    @pl.loop(1, PLANE)
    def _(d):
        plane_copy(d).start()

    plane_in[yc] = plane_out[yc]

    @pl.loop(1, PLANE)
    def _(d):
        plane_arrival(d).wait_recv()

    to_row = lax.broadcasted_iota(jnp.int32, (slots, slots), 0)
    from_row = lax.broadcasted_iota(jnp.int32, (slots, slots), 1)
    by_ring = ((to_row >> 1) & (PLANE - 1)) * (2 * RING) + (to_row >> 4) * 2 + (to_row & 1)
    by_ring = (by_ring == from_row).astype(jnp.float32).astype(jnp.bfloat16)
    by_plane = ((to_row >> 1) & (RING - 1)) * (2 * PLANE) + (to_row >> 5) * 2 + (to_row & 1)
    by_plane = (by_plane == from_row).astype(jnp.float32).astype(jnp.bfloat16)
    ordered = dot(by_ring, plane_in[...].reshape(slots, PART)).astype(jnp.bfloat16)
    ring_out[...] = ordered.reshape(RING, 2 * PLANE, PART)

    def ring_copy(d):
        to = (z + d) % RING
        return remote(
            ring_out.at[to], box.at[x, z], s_ring.at[d], r_ring.at[d], to * PLANE + yc, x
        )

    def ring_arrival(d):
        return remote(
            ring_out.at[z],
            box.at[x, (z + RING - d) % RING],
            s_ring.at[d],
            r_ring.at[d],
            me,
            (x + 1) % LANES,
        )

    def box_copy(d, j):
        at = (z + RING - d) % RING
        return remote(
            box.at[x, at],
            box.at[x, at],
            s_box.at[d, j - 1],
            r_box.at[d, j - 1],
            me,
            (x + j) % LANES,
        )

    def box_arrival(d, j):
        at = (z + RING - d) % RING
        return remote(
            box.at[x, at],
            box.at[(x + LANES - j) % LANES, at],
            s_box.at[d, j - 1],
            r_box.at[d, j - 1],
            me,
            (x + j) % LANES,
        )

    @pl.loop(0, RING - 1)
    def _(t):
        ring_copy(far_first(t)).start()

    box[x, z] = ring_out[z]
    for j in range(1, LANES):
        box_copy(0, j).start()

    @pl.loop(0, RING - 1)
    def _(t):
        d = far_first(t)
        ring_arrival(d).wait_recv()
        for j in range(1, LANES):
            box_copy(d, j).start()

    @pl.loop(0, RING)
    def _(d):
        for j in range(1, LANES):
            box_arrival(d, j).wait_recv()

    for load in loads[4:]:
        load.wait()
    gate_val = jnp.zeros((slots, gate.shape[0]), jnp.float32)
    up_val = jnp.zeros((slots, gate.shape[0]), jnp.float32)
    for j in range(LANES):
        part = box[j].reshape(slots, PART)
        gate_val = gate_val + dot_t(part, gate[:, j * PART : (j + 1) * PART])
        up_val = up_val + dot_t(part, up[:, j * PART : (j + 1) * PART])
    hidden = (jnp.maximum(gate_val, 0.0) * up_val).astype(jnp.bfloat16)
    for j in range(LANES):
        product = dot(hidden, down[:, j * PART : (j + 1) * PART]).astype(jnp.bfloat16)
        partial[j] = product.reshape(RING, 2 * PLANE, PART)

    def part_copy(d, j):
        at = (z + d) % RING
        to = (x + j) % LANES
        return remote(
            partial.at[to, at],
            partial_in.at[j - 1, at],
            s_part.at[d, j - 1],
            r_part.at[d, j - 1],
            me,
            to,
        )

    def sum_copy(d):
        to = (z + d) % RING
        return remote(sums.at[to], sums_in.at[z], s_sum.at[d], r_sum.at[d], to * PLANE + yc, x)

    def sum_arrival(d):
        return remote(
            sums.at[z],
            sums_in.at[(z + RING - d) % RING],
            s_sum.at[d],
            r_sum.at[d],
            me,
            (x + 1) % LANES,
        )

    @pl.loop(0, RING)
    def _(t):
        for j in range(1, LANES):
            part_copy(far_first(t), j).start()

    def add_parts(d):
        at = (z + d) % RING
        value = partial[x, at].astype(jnp.float32)
        for j in range(1, LANES):
            part_copy(d, j).wait_recv()
            value = value + partial_in[j - 1, at].astype(jnp.float32)
        return value.astype(jnp.bfloat16)

    @pl.loop(0, RING - 1)
    def _(t):
        d = far_first(t)
        sums[(z + d) % RING] = add_parts(d)
        sum_copy(d).start()

    sums_in[z] = add_parts(0)

    @pl.loop(1, RING)
    def _(d):
        sum_arrival(d).wait_recv()

    ordered = dot(by_plane, sums_in[...].reshape(slots, PART)).astype(jnp.bfloat16)
    back_out[...] = ordered.reshape(PLANE, 2 * RING, PART)

    def back_copy(d):
        to = (yc + d) % PLANE
        return remote(
            back_out.at[to], back_in.at[yc], s_back.at[d], r_back.at[d], z * PLANE + to, x
        )

    def back_arrival(d):
        return remote(
            back_out.at[yc],
            back_in.at[(yc + PLANE - d) % PLANE],
            s_back.at[d],
            r_back.at[d],
            me,
            (x + 1) % LANES,
        )

    @pl.loop(1, PLANE)
    def _(d):
        back_copy(d).start()

    back_in[yc] = back_out[yc]
    high = weigh.astype(jnp.bfloat16)
    low = (weigh - high.astype(jnp.float32)).astype(jnp.bfloat16)

    @pl.loop(1, PLANE)
    def _(d):
        back_arrival(d).wait_recv()

    returned = back_in[...].reshape(slots, PART)
    combined = residual + (t_dot(high, returned) + t_dot(low, returned))
    total = whole_square(combined, 1)
    final = as_row(final_ref[...]).astype(jnp.float32)
    out_ref[...] = (combined * lax.rsqrt(total / width + EPSILON) * final).astype(out_ref.dtype)

    new_copy.wait_send()
    cache_copy.wait_send()
    for d in range(1, LANES):
        att_copy(d).wait_send()

    @pl.loop(1, PLANE)
    def _(d):
        plane_copy(d).wait_send()
        back_copy(d).wait_send()

    @pl.loop(1, RING)
    def _(d):
        ring_copy(d).wait_send()
        sum_copy(d).wait_send()

    @pl.loop(0, RING)
    def _(d):
        for j in range(1, LANES):
            box_copy(d, j).wait_send()
            part_copy(d, j).wait_send()


def layer_call(small, large):
    rows = small[0].shape[0]
    vmem, sem = pltpu.VMEM, pltpu.SemaphoreType.DMA
    bf16 = jnp.bfloat16
    by_plane = vmem((PLANE, 2 * RING, PART), bf16)
    by_ring = vmem((RING, 2 * PLANE, PART), bf16)
    held = [vmem(block.shape, bf16) for block in large]
    held[2] = vmem((2, CACHE, HEAD), bf16)
    return pl.pallas_call(
        layer_kernel,
        out_shape=jax.ShapeDtypeStruct((rows, PART), bf16),
        in_specs=[pl.BlockSpec(memory_space=pltpu.VMEM)] * len(small)
        + [pl.BlockSpec(memory_space=pl.ANY)] * len(large),
        out_specs=pl.BlockSpec(memory_space=pltpu.VMEM),
        scratch_shapes=held
        + [
            vmem((2, rows, HEAD), bf16),
            vmem((LANES, rows, PART), bf16),
            vmem((LANES - 1, rows, PART), bf16),
            vmem((2, rows, 128), jnp.float32),
            vmem((2, LANES - 1, rows, 128), jnp.float32),
            by_plane,
            by_plane,
            by_ring,
            vmem((LANES, RING, 2 * PLANE, PART), bf16),
            vmem((LANES, RING, 2 * PLANE, PART), bf16),
            vmem((LANES - 1, RING, 2 * PLANE, PART), bf16),
            by_ring,
            by_ring,
            by_plane,
            by_plane,
        ]
        + [sem((LANES - 1,))] * 2
        + [sem((2, LANES - 1))] * 2
        + [sem((PLANE,))] * 2
        + [sem((RING,))] * 2
        + [sem((RING, LANES - 1))] * 4
        + [sem((RING,))] * 2
        + [sem((PLANE,))] * 2
        + [sem((2,))] * 2
        + [sem((7,))],
        compiler_params=pltpu.CompilerParams(collective_id=0, has_side_effects=True),
    )(*small, *large)


def on_device(
    tokens,
    attn_gain,
    query_weight,
    key_value_weight,
    paired_cache,
    prompt_length,
    group_index,
    offsets,
    sink_logit,
    out_weight,
    mixer_gain,
    routes,
    route_weight,
    copy_slot,
    gate_weight,
    up_weight,
    down_weight,
    final_gain,
):
    half = HEAD // 2
    frequency = 10000.0 ** (-np.arange(half, dtype=np.float64) / half)
    frequency = jnp.asarray(np.tile(frequency, 2)[None, :], jnp.float32)
    small = [
        tokens,
        attn_gain,
        prompt_length,
        group_index.reshape(1, -1),
        offsets.reshape(1, -1),
        sink_logit.reshape(1, -1),
        frequency,
        mixer_gain,
        routes.T,
        route_weight.T,
        copy_slot.reshape(1, -1),
        final_gain,
    ]
    large = [
        query_weight,
        key_value_weight[0],
        paired_cache[0, 0],
        out_weight,
        gate_weight[0].T,
        up_weight[0].T,
        down_weight[0],
    ]
    return layer_call(small, large)


def solution(mesh):
    in_specs = (
        P("expert", None),
        P(),
        P(None, "tensor"),
        P("tensor", None, None),
        P("expert", "tensor", None, None),
        P("expert", None),
        P("expert"),
        P("expert"),
        P("tensor"),
        P("tensor", None),
        P(),
        P("expert", None),
        P("expert", None),
        P(),
        P("expert", None, "tensor"),
        P("expert", None, "tensor"),
        P("expert", "tensor", None),
        P("tensor"),
    )
    out_specs = P("expert", "tensor")
    return jax.shard_map(
        on_device, mesh=mesh, in_specs=in_specs, out_specs=out_specs, check_vma=False
    )
```

```python
import jax
import jax.numpy as jnp
import numpy as np
from jax import lax
from jax.experimental import pallas as pl
from jax.experimental.pallas import tpu as pltpu
from jax.sharding import PartitionSpec as P

EXPERTS = 32
TOP = 4
PROMPT_CAP = 256
WINDOW = 192


EPSILON = 1e-06


def rms_scale(values, gain_row):
    mean_square = jnp.mean(values * values, axis=-1, keepdims=True)
    return values * lax.rsqrt(mean_square + EPSILON) * gain_row.astype(jnp.float32)


RING = 16
PLANE = 8
LANES = 4
PART = 384
HEAD = 128
HEADS = 3
CACHE = 768
MESH = pl.DeviceIdType.MESH


def far_first(t):
    half = (t + 1) // 2
    return RING // 2 + half * (1 - 2 * (t % 2))


def remote(src, dst, send, recv, expert, tensor):
    return pltpu.make_async_remote_copy(
        src_ref=src,
        dst_ref=dst,
        send_sem=send,
        recv_sem=recv,
        device_id=(expert, tensor),
        device_id_type=MESH,
    )


def dot(a, b):
    return jnp.dot(a, b, preferred_element_type=jnp.float32)


def dot_t(a, b):
    return lax.dot_general(a, b, (((1,), (1,)), ((), ())), preferred_element_type=jnp.float32)


def as_row(values):
    return values.astype(jnp.float32).reshape(1, -1)


def t_dot(a, b):
    return lax.dot_general(a, b, (((0,), (0,)), ((), ())), preferred_element_type=jnp.float32)


def layer_kernel(
    tokens_ref,
    attn_gain_ref,
    length_ref,
    group_ref,
    offset_ref,
    sink_ref,
    frequency_ref,
    mixer_ref,
    routes_ref,
    route_weight_ref,
    copy_slot_ref,
    final_ref,
    query_weight_hbm,
    kv_weight_hbm,
    cache_hbm,
    out_weight_hbm,
    gate_hbm,
    up_hbm,
    down_hbm,
    out_ref,
    query_weight,
    kv_weight,
    cache,
    out_weight,
    gate,
    up,
    down,
    new_kv,
    att,
    att_in,
    sq,
    sq_in,
    plane_out,
    plane_in,
    ring_out,
    box,
    partial,
    partial_in,
    sums,
    sums_in,
    back_out,
    back_in,
    s_att,
    r_att,
    s_sq,
    r_sq,
    s_plane,
    r_plane,
    s_ring,
    r_ring,
    s_box,
    r_box,
    s_part,
    r_part,
    s_sum,
    r_sum,
    s_back,
    r_back,
    s_kv,
    r_kv,
    s_load,
):
    me = lax.axis_index("expert")
    x = lax.axis_index("tensor")
    z = me // PLANE
    yc = me % PLANE
    rows = tokens_ref.shape[0]
    width = LANES * PART

    barrier = pltpu.get_barrier_semaphore()

    def greet(expert, tensor):
        pl.semaphore_signal(barrier, inc=1, device_id=(expert, tensor), device_id_type=MESH)

    @pl.loop(1, RING)
    def _(d):
        greet((z + d) % RING * PLANE + yc, x)

    @pl.loop(1, PLANE)
    def _(d):
        greet(z * PLANE + (yc + d) % PLANE, x)

    @pl.loop(1, LANES)
    def _(d):
        greet(me, (x + d) % LANES)

    half = x % 2
    loads = [
        pltpu.make_async_copy(src, dst, s_load.at[i])
        for i, (src, dst) in enumerate(
            [
                (query_weight_hbm, query_weight),
                (kv_weight_hbm, kv_weight),
                (cache_hbm, cache.at[half]),
                (out_weight_hbm, out_weight),
                (gate_hbm, gate),
                (up_hbm, up),
                (down_hbm, down),
            ]
        )
    ]
    for load in loads:
        load.start()

    slots = 2 * RING * PLANE
    copies = copy_slot_ref.shape[1]
    replicas = copies // EXPERTS
    group_rows = rows // replicas
    early = lax.broadcasted_iota(jnp.int32, (rows, rows), 0)
    late = lax.broadcasted_iota(jnp.int32, (rows, rows), 1)
    before = (early // group_rows == late // group_rows) & (early < late)
    before = before.astype(jnp.float32).astype(jnp.bfloat16)
    expert_row = lax.broadcasted_iota(jnp.int32, (EXPERTS, rows), 0)
    named = [
        (routes_ref[k : k + 1, :] == expert_row).astype(jnp.float32) for k in range(TOP)
    ]
    earlier = dot(sum(named).astype(jnp.bfloat16), before)
    copy_row = lax.broadcasted_iota(jnp.int32, (copies, rows), 0)
    row_block = lax.broadcasted_iota(jnp.int32, (1, rows), 1) // group_rows
    slot_of = jnp.broadcast_to(copy_slot_ref[...].astype(jnp.float32), (16, copies))
    slot_of = slot_of.astype(jnp.bfloat16)
    place_row = lax.broadcasted_iota(jnp.int32, (slots, rows), 0)
    taken = jnp.zeros((slots, rows), jnp.float32)
    weigh = jnp.zeros((slots, rows), jnp.float32)
    for k in range(TOP):
        rank = jnp.sum(named[k] * earlier, axis=0, keepdims=True).astype(jnp.int32)
        wanted = routes_ref[k : k + 1, :] * replicas + row_block
        picks = (wanted == copy_row).astype(jnp.float32).astype(jnp.bfloat16)
        holder = dot(slot_of, picks)[:1].astype(jnp.int32)
        place = (holder & (PLANE - 1)) * (2 * RING) + (holder >> 3) * 2 + rank
        hit = place == place_row
        taken = taken + hit.astype(jnp.float32)
        weigh = weigh + jnp.where(hit, route_weight_ref[k : k + 1, :], 0.0)

    values = tokens_ref[...].astype(jnp.float32)
    normed_in = rms_scale(values, as_row(attn_gain_ref[...])).astype(jnp.bfloat16)

    def column(row):
        return jnp.sum(jnp.where(early == late, row.astype(jnp.float32), 0.0), axis=1, keepdims=True)

    group = column(group_ref[...])
    row_length = jnp.zeros((rows, 1), jnp.float32)
    for p in range(length_ref.shape[1]):
        this = length_ref[:, p : p + 1].astype(jnp.float32)
        row_length = row_length + jnp.where(group == p, this, 0.0)
    position = row_length + column(offset_ref[...])
    angles = position * frequency_ref[...]
    lane = lax.broadcasted_iota(jnp.int32, angles.shape, 1)
    cosine = jnp.cos(angles)
    sine = jnp.where(lane < HEAD // 2, -jnp.sin(angles), jnp.sin(angles))
    loads[2].wait()
    pl.semaphore_wait(barrier, RING + PLANE + LANES - 3)
    partner = x + 1 - 2 * half
    cache_copy = remote(cache.at[half], cache.at[half], s_kv.at[1], r_kv.at[1], me, partner)
    cache_copy.start()
    loads[0].wait()
    loads[1].wait()
    queries = dot(normed_in, query_weight[...])
    heads = []
    for h in range(HEADS):
        one = queries[:, h * HEAD : (h + 1) * HEAD]
        heads.append(one * cosine + pltpu.roll(one, HEAD // 2, 1) * sine)
    queries = jnp.concatenate(heads, axis=0).astype(jnp.bfloat16)
    projected = dot(normed_in, kv_weight[...])
    turned = projected * cosine + pltpu.roll(projected, HEAD // 2, 1) * sine
    marks_key = lane * 0 + half == 0
    new_kv[half] = jnp.where(marks_key, turned, projected).astype(jnp.bfloat16)
    new_copy = remote(
        new_kv.at[half], new_kv.at[half], s_kv.at[0], r_kv.at[0], me, partner
    )
    new_arrival = remote(
        new_kv.at[half], new_kv.at[1 - half], s_kv.at[0], r_kv.at[0], me, partner
    )
    cache_arrival = remote(
        cache.at[half], cache.at[1 - half], s_kv.at[1], r_kv.at[1], me, partner
    )
    new_copy.start()

    def stacked(block):
        return jnp.concatenate([block] * HEADS, axis=0)

    total_rows = HEADS * rows
    scale = HEAD**-0.5
    slot = lax.broadcasted_iota(jnp.int32, (rows, CACHE), 1)
    slot_pos = (slot & (PROMPT_CAP - 1)).astype(jnp.float32)
    visible = (
        ((slot >> 8).astype(jnp.float32) == group)
        & (slot_pos < row_length)
        & (slot_pos > position - WINDOW)
    )
    visible = stacked(jnp.where(visible, 1.0, 0.0)) > 0.5
    sinks = jnp.concatenate(
        [jnp.broadcast_to(sink_ref[:, h : h + 1], (rows, 1)) for h in range(HEADS)], axis=0
    )
    new_arrival.wait_recv()
    new_key = stacked(new_kv[0].astype(jnp.float32))
    new_value = stacked(new_kv[1].astype(jnp.float32))
    self_score = jnp.sum(queries.astype(jnp.float32) * new_key, axis=1, keepdims=True) * scale
    cache_arrival.wait_recv()
    scores = dot_t(queries, cache[0]) * scale
    ceiling = jnp.max(jnp.where(visible, scores, -jnp.inf), axis=1, keepdims=True)
    ceiling = jnp.maximum(jnp.maximum(ceiling, self_score), sinks)
    weights = jnp.where(visible, jnp.exp(scores - ceiling), 0.0)
    own_weight = jnp.exp(self_score - ceiling)
    denominator = (
        jnp.sum(weights, axis=1, keepdims=True) + own_weight + jnp.exp(sinks - ceiling)
    )
    probabilities = (weights / denominator).astype(jnp.bfloat16)
    own_prob = (own_weight / denominator).astype(jnp.bfloat16).astype(jnp.float32)
    context = dot(probabilities, cache[1]) + own_prob * new_value
    context = context.astype(jnp.bfloat16)
    context = jnp.concatenate(
        [context[h * rows : (h + 1) * rows] for h in range(HEADS)], axis=1
    )
    loads[3].wait()

    for j in range(LANES):
        att[j] = dot(context, out_weight[:, j * PART : (j + 1) * PART]).astype(jnp.bfloat16)

    def att_copy(d):
        to = (x + d) % LANES
        return remote(att.at[to], att_in.at[d - 1], s_att.at[d - 1], r_att.at[d - 1], me, to)

    for d in range(1, LANES):
        att_copy(d).start()
    mine = pl.ds(pl.multiple_of(x * PART, 128), PART)
    summed = att[x].astype(jnp.float32)
    for d in range(1, LANES):
        att_copy(d).wait_recv()
        summed = summed + att_in[d - 1].astype(jnp.float32)
    summed = summed.astype(jnp.bfloat16).astype(jnp.float32)
    residual = (tokens_ref[:, mine].astype(jnp.float32) + summed).astype(jnp.bfloat16)
    residual = residual.astype(jnp.float32)

    def whole_square(values, which):
        own = jnp.sum(values * values, axis=1, keepdims=True)
        sq[which] = jnp.broadcast_to(own, (rows, 128))

        def copy(d):
            to = (x + d) % LANES
            return remote(
                sq.at[which],
                sq_in.at[which, d - 1],
                s_sq.at[which, d - 1],
                r_sq.at[which, d - 1],
                me,
                to,
            )

        for d in range(1, LANES):
            copy(d).start()
        total = own
        for d in range(1, LANES):
            copy(d).wait_recv()
            total = total + sq_in[which, d - 1][:, :1]
        for d in range(1, LANES):
            copy(d).wait_send()
        return total

    total = whole_square(residual, 0)
    gains = as_row(mixer_ref[...])
    gain = jnp.zeros((1, PART), jnp.float32)
    for j in range(LANES):
        this = (x == j).astype(jnp.float32)
        gain = gain + this * gains[:, j * PART : (j + 1) * PART]
    mixed = (residual * lax.rsqrt(total / width + EPSILON) * gain).astype(jnp.bfloat16)

    outbox = dot(taken.astype(jnp.bfloat16), mixed).astype(jnp.bfloat16)
    plane_out[...] = outbox.reshape(PLANE, 2 * RING, PART)

    def plane_copy(d):
        to = (yc + d) % PLANE
        return remote(
            plane_out.at[to], plane_in.at[yc], s_plane.at[d], r_plane.at[d], z * PLANE + to, x
        )

    def plane_arrival(d):
        return remote(
            plane_out.at[yc],
            plane_in.at[(yc + PLANE - d) % PLANE],
            s_plane.at[d],
            r_plane.at[d],
            me,
            (x + 1) % LANES,
        )

    @pl.loop(1, PLANE)
    def _(d):
        plane_copy(d).start()

    plane_in[yc] = plane_out[yc]

    @pl.loop(1, PLANE)
    def _(d):
        plane_arrival(d).wait_recv()

    to_row = lax.broadcasted_iota(jnp.int32, (slots, slots), 0)
    from_row = lax.broadcasted_iota(jnp.int32, (slots, slots), 1)
    by_ring = ((to_row >> 1) & (PLANE - 1)) * (2 * RING) + (to_row >> 4) * 2 + (to_row & 1)
    by_ring = (by_ring == from_row).astype(jnp.float32).astype(jnp.bfloat16)
    by_plane = ((to_row >> 1) & (RING - 1)) * (2 * PLANE) + (to_row >> 5) * 2 + (to_row & 1)
    by_plane = (by_plane == from_row).astype(jnp.float32).astype(jnp.bfloat16)
    ordered = dot(by_ring, plane_in[...].reshape(slots, PART)).astype(jnp.bfloat16)
    ring_out[...] = ordered.reshape(RING, 2 * PLANE, PART)

    def ring_copy(d):
        to = (z + d) % RING
        return remote(
            ring_out.at[to], box.at[x, z], s_ring.at[d], r_ring.at[d], to * PLANE + yc, x
        )

    def ring_arrival(d):
        return remote(
            ring_out.at[z],
            box.at[x, (z + RING - d) % RING],
            s_ring.at[d],
            r_ring.at[d],
            me,
            (x + 1) % LANES,
        )

    def box_copy(d, j):
        at = (z + RING - d) % RING
        return remote(
            box.at[x, at],
            box.at[x, at],
            s_box.at[d, j - 1],
            r_box.at[d, j - 1],
            me,
            (x + j) % LANES,
        )

    def box_arrival(d, j):
        at = (z + RING - d) % RING
        return remote(
            box.at[x, at],
            box.at[(x + LANES - j) % LANES, at],
            s_box.at[d, j - 1],
            r_box.at[d, j - 1],
            me,
            (x + j) % LANES,
        )

    @pl.loop(0, RING - 1)
    def _(t):
        ring_copy(far_first(t)).start()

    box[x, z] = ring_out[z]
    for j in range(1, LANES):
        box_copy(0, j).start()

    @pl.loop(0, RING - 1)
    def _(t):
        d = far_first(t)
        ring_arrival(d).wait_recv()
        for j in range(1, LANES):
            box_copy(d, j).start()

    @pl.loop(0, RING)
    def _(d):
        for j in range(1, LANES):
            box_arrival(d, j).wait_recv()

    for load in loads[4:]:
        load.wait()
    gate_val = jnp.zeros((slots, gate.shape[0]), jnp.float32)
    up_val = jnp.zeros((slots, gate.shape[0]), jnp.float32)
    for j in range(LANES):
        part = box[j].reshape(slots, PART)
        gate_val = gate_val + dot_t(part, gate[:, j * PART : (j + 1) * PART])
        up_val = up_val + dot_t(part, up[:, j * PART : (j + 1) * PART])
    hidden = (jnp.maximum(gate_val, 0.0) * up_val).astype(jnp.bfloat16)
    for j in range(LANES):
        product = dot(hidden, down[:, j * PART : (j + 1) * PART]).astype(jnp.bfloat16)
        partial[j] = product.reshape(RING, 2 * PLANE, PART)

    def part_copy(d, j):
        at = (z + d) % RING
        to = (x + j) % LANES
        return remote(
            partial.at[to, at],
            partial_in.at[j - 1, at],
            s_part.at[d, j - 1],
            r_part.at[d, j - 1],
            me,
            to,
        )

    def sum_copy(d):
        to = (z + d) % RING
        return remote(sums.at[to], sums_in.at[z], s_sum.at[d], r_sum.at[d], to * PLANE + yc, x)

    def sum_arrival(d):
        return remote(
            sums.at[z],
            sums_in.at[(z + RING - d) % RING],
            s_sum.at[d],
            r_sum.at[d],
            me,
            (x + 1) % LANES,
        )

    @pl.loop(0, RING)
    def _(t):
        for j in range(1, LANES):
            part_copy(far_first(t), j).start()

    def add_parts(d):
        at = (z + d) % RING
        value = partial[x, at].astype(jnp.float32)
        for j in range(1, LANES):
            part_copy(d, j).wait_recv()
            value = value + partial_in[j - 1, at].astype(jnp.float32)
        return value.astype(jnp.bfloat16)

    @pl.loop(0, RING - 1)
    def _(t):
        d = far_first(t)
        sums[(z + d) % RING] = add_parts(d)
        sum_copy(d).start()

    sums_in[z] = add_parts(0)

    @pl.loop(1, RING)
    def _(d):
        sum_arrival(d).wait_recv()

    ordered = dot(by_plane, sums_in[...].reshape(slots, PART)).astype(jnp.bfloat16)
    back_out[...] = ordered.reshape(PLANE, 2 * RING, PART)

    def back_copy(d):
        to = (yc + d) % PLANE
        return remote(
            back_out.at[to], back_in.at[yc], s_back.at[d], r_back.at[d], z * PLANE + to, x
        )

    def back_arrival(d):
        return remote(
            back_out.at[yc],
            back_in.at[(yc + PLANE - d) % PLANE],
            s_back.at[d],
            r_back.at[d],
            me,
            (x + 1) % LANES,
        )

    @pl.loop(1, PLANE)
    def _(d):
        back_copy(d).start()

    back_in[yc] = back_out[yc]
    high = weigh.astype(jnp.bfloat16)
    low = (weigh - high.astype(jnp.float32)).astype(jnp.bfloat16)

    @pl.loop(1, PLANE)
    def _(d):
        back_arrival(d).wait_recv()

    returned = back_in[...].reshape(slots, PART)
    combined = residual + (t_dot(high, returned) + t_dot(low, returned))
    total = whole_square(combined, 1)
    final = as_row(final_ref[...]).astype(jnp.float32)
    out_ref[...] = (combined * lax.rsqrt(total / width + EPSILON) * final).astype(out_ref.dtype)

    new_copy.wait_send()
    cache_copy.wait_send()
    for d in range(1, LANES):
        att_copy(d).wait_send()

    @pl.loop(1, PLANE)
    def _(d):
        plane_copy(d).wait_send()
        back_copy(d).wait_send()

    @pl.loop(1, RING)
    def _(d):
        ring_copy(d).wait_send()
        sum_copy(d).wait_send()

    @pl.loop(0, RING)
    def _(d):
        for j in range(1, LANES):
            box_copy(d, j).wait_send()
            part_copy(d, j).wait_send()


def layer_call(small, large):
    rows = small[0].shape[0]
    vmem, sem = pltpu.VMEM, pltpu.SemaphoreType.DMA
    bf16 = jnp.bfloat16
    by_plane = vmem((PLANE, 2 * RING, PART), bf16)
    by_ring = vmem((RING, 2 * PLANE, PART), bf16)
    held = [vmem(block.shape, bf16) for block in large]
    held[2] = vmem((2, CACHE, HEAD), bf16)
    return pl.pallas_call(
        layer_kernel,
        out_shape=jax.ShapeDtypeStruct((rows, PART), bf16),
        in_specs=[pl.BlockSpec(memory_space=pltpu.VMEM)] * len(small)
        + [pl.BlockSpec(memory_space=pl.ANY)] * len(large),
        out_specs=pl.BlockSpec(memory_space=pltpu.VMEM),
        scratch_shapes=held
        + [
            vmem((2, rows, HEAD), bf16),
            vmem((LANES, rows, PART), bf16),
            vmem((LANES - 1, rows, PART), bf16),
            vmem((2, rows, 128), jnp.float32),
            vmem((2, LANES - 1, rows, 128), jnp.float32),
            by_plane,
            by_plane,
            by_ring,
            vmem((LANES, RING, 2 * PLANE, PART), bf16),
            vmem((LANES, RING, 2 * PLANE, PART), bf16),
            vmem((LANES - 1, RING, 2 * PLANE, PART), bf16),
            by_ring,
            by_ring,
            by_plane,
            by_plane,
        ]
        + [sem((LANES - 1,))] * 2
        + [sem((2, LANES - 1))] * 2
        + [sem((PLANE,))] * 2
        + [sem((RING,))] * 2
        + [sem((RING, LANES - 1))] * 4
        + [sem((RING,))] * 2
        + [sem((PLANE,))] * 2
        + [sem((2,))] * 2
        + [sem((7,))],
        compiler_params=pltpu.CompilerParams(collective_id=0, has_side_effects=True),
    )(*small, *large)


def on_device(
    tokens,
    attn_gain,
    query_weight,
    key_value_weight,
    paired_cache,
    prompt_length,
    group_index,
    offsets,
    sink_logit,
    out_weight,
    mixer_gain,
    routes,
    route_weight,
    copy_slot,
    gate_weight,
    up_weight,
    down_weight,
    final_gain,
):
    half = HEAD // 2
    frequency = 10000.0 ** (-np.arange(half, dtype=np.float64) / half)
    frequency = jnp.asarray(np.tile(frequency, 2)[None, :], jnp.float32)
    small = [
        tokens,
        attn_gain,
        prompt_length,
        group_index.reshape(1, -1),
        offsets.reshape(1, -1),
        sink_logit.reshape(1, -1),
        frequency,
        mixer_gain,
        routes.T,
        route_weight.T,
        copy_slot.reshape(1, -1),
        final_gain,
    ]
    large = [
        query_weight,
        key_value_weight[0],
        paired_cache[0, 0],
        out_weight,
        gate_weight[0].T,
        up_weight[0].T,
        down_weight[0],
    ]
    return layer_call(small, large)


def solution(mesh):
    in_specs = (
        P("expert", None),
        P(),
        P(None, "tensor"),
        P("tensor", None, None),
        P("expert", "tensor", None, None),
        P("expert", None),
        P("expert"),
        P("expert"),
        P("tensor"),
        P("tensor", None),
        P(),
        P("expert", None),
        P("expert", None),
        P(),
        P("expert", None, "tensor"),
        P("expert", None, "tensor"),
        P("expert", "tensor", None),
        P("tensor"),
    )
    out_specs = P("expert", "tensor")
    return jax.shard_map(
        on_device, mesh=mesh, in_specs=in_specs, out_specs=out_specs, check_vma=False
    )
```
